32 devices in a mesh: groups: 2 (over y), wide: 4 (over z), planes: 2 (over x), rep: 2 (over core).
Axes of the slice: x: 2, y: 2, z: 4, core: 2. Of those that a mesh axis runs over, the one named last changes fastest.
Arguments:
- movie_frames: bfloat16 [4, 128, 256, 128], P('planes', ('groups', 'wide'), 'rep'), parts along dimension 1, may hold values from -6 to 6
- pixel_mask: int32 [256, 128], P('rep'), may hold values 0 or 1
- tile_owner: int32 [256, 1], P('rep'), may hold values from 0 to 3; in each aligned block of 128 rows (0 to 127, 128 to 255, ...) at most 48 rows name the same one
- support: int32 [256, 128], P('rep'), may hold values from 0 to 511
- templates: bfloat16 [512, 4, 128], P(None, 'planes'), may hold values from -0.25 to 0.25
- row_taps: float32 [25], replicated, may hold values from -1.25 to 1.25
- col_taps: float32 [25], replicated, may hold values from -1.25 to 1.25
- lag_gains: float32 [4, 3, 65], P('wide'), may hold values from -0.4375 to 0.4375
- dilations: int32 [4, 3], P('wide'), may hold values from 1 to 8
Outputs:
- traces: bfloat16 [128, 128, 256], P('planes', ('groups', 'wide'), 'rep'), parts along dimension 1
- back_projected: bfloat16 [4, 128, 256, 128], P('planes', ('groups', 'wide'), 'rep'), parts along dimension 1
The draws below stay inside these ranges and needn't reach their ends.
There are 2 independent parts, one for each index of `groups`. The reference program is written for one: setup_inputs(seed, part) draws one part's arguments, and reference() takes and returns one part's arrays. A program takes and returns all parts, laid end to end along the dimension named above; an argument that names none is the same for every part. Nothing has to cross between parts.
Inputs may be any that keep to these rules, and one draw needn't show every extreme that they name: Strip h belongs to region class tile_owner[h,0]; the 128 rows of one device name each class at most 48 times.
All inputs are finite; a program needn't handle non-finite values. No bound on the sum of `pixel_mask` on one device may be relied on, other than what follows from the above.
Results may differ from the reference program's by a relative error of at most 0.015.
Values may be sent and summed in bfloat16 or wider, within the bound.
A program may use at most 64 MiB of HBM per device.

```python
import math
import jax
import jax.numpy as jnp
import numpy as np
from jax import lax

H = 256
W = 128
FP = 128
NCOMP = 512
TAPS_S = 25
TAPS_T = 65
BANDS = 3
DMAX = 8
PLANES = 4
FRAMES = 64
HH = 128
CLUSTERS = 4
CAP = 48
N_REP = 2


def place_ends(entries, stream_key, least, high):
    longest = entries.shape.index(max(entries.shape))
    spots = []
    for shift in (0, 1):
        where = [jax.random.randint(jax.random.fold_in(stream_key, axis), (), 0, length) for axis, length in enumerate(entries.shape)]
        where[longest] = (where[longest] + shift) % entries.shape[longest]
        spots.append(tuple(where))
    return entries.at[spots[0]].set(least).at[spots[1]].set(high)


def level_of(key, shape, shards, smallest, top_value):
    def one(position, shards_of):
        draws = jax.random.uniform(jax.random.fold_in(jax.random.fold_in(key, 6), position), (shards_of,), jnp.float32, smallest / len(shards), top_value / len(shards))
        return jnp.repeat(jnp.exp(draws), shape[position] // shards_of).reshape((-1,) + (1,) * (len(shape) - position - 1))

    factor_of = one(*shards[0])
    for cut in shards[1:]:
        factor_of = factor_of * one(*cut)
    return factor_of


def deal_out(stream_key, own, number, rows, count, top, most, slope):
    sequence = jax.random.permutation(stream_key, count)
    packed, ordinary = load_shares(count, rows * top, most, slope, True), load_shares(count, rows * top, most, slope, False)
    places = jnp.arange(count)

    def named(tallies, offset_by):
        used = int((tallies > 0).sum())
        fixed = max(1, used // 4)
        passed = fixed + (places - fixed + offset_by * (used - fixed)) % max(1, count - fixed)
        return jnp.zeros((count,), jnp.int32).at[sequence[jnp.where(places < fixed, places, passed)]].set(jnp.asarray(tallies, jnp.int32))

    tallies = jnp.where(number % 4 == 0, named(packed, number // 4), named(ordinary, number - number // 4 - 1))
    mixed = jax.random.permutation(jax.random.fold_in(own, 3), count)
    donor, taker = mixed[0:count // 2 * 2:2], mixed[1:count // 2 * 2:2]
    room = jnp.minimum(tallies[donor] - 1, most - tallies[taker]) // 2
    room = jnp.where((donor == sequence[0]) | (taker == sequence[0]) | (tallies[taker] == 0), 0, jnp.maximum(room, 0))
    passed = jax.random.randint(jax.random.fold_in(own, 4), (count // 2,), 0, 1 << 20) % (room + 1)
    tallies = tallies.at[donor].add(-passed).at[taker].add(passed)
    items = jnp.searchsorted(jnp.cumsum(tallies), jnp.arange(rows * top), side="right").astype(jnp.int32)
    grid = items.reshape(top, rows).T
    grid = grid[jax.random.permutation(jax.random.fold_in(own, 1), rows)]
    offset_by = jax.random.randint(jax.random.fold_in(own, 2), (rows, 1), 0, top)
    return jnp.take_along_axis(grid, (jnp.arange(top)[None, :] + offset_by) % top, axis=1)


def load_shares(number_of, total, most, lean, full):
    weights = [(1 << 20) // math.isqrt(grade ** lean) + 1 for grade in range(1, number_of + 1)]
    largest = most if full else min(most, max(-(-total // number_of), total * weights[0] // sum(weights)))
    least = 1 if total - largest >= number_of - 1 else 0
    holding, spare = [largest] + [least] * (number_of - 1), total - largest - least * (number_of - 1)
    while spare > 0:
        free = [i for i in range(1, number_of) if holding[i] < largest] or [i for i in range(1, number_of) if holding[i] < most]
        pool, remaining = sum([weights[i] for i in free]), spare
        for i in free:
            addition = min(most - holding[i], max(1, remaining * weights[i] // pool), spare)
            holding[i] = holding[i] + addition
            spare = spare - addition
    return np.array(holding)


def normal_values(rng, extent, scale, reach, shards=(), held_as=jnp.bfloat16):
    values = scale * jax.random.normal(rng, extent, jnp.float32)
    if shards:
        values = values * level_of(rng, extent, shards, -0.22, 0.18)
    return jnp.clip(values, -reach, reach).astype(held_as)


def setup_inputs(seed: int = 0, part: int = 0) -> dict:
    key_list = jax.random.split(jax.random.key(seed), 10)
    own_keys = jax.random.split(jax.random.fold_in(key_list[9], part), 10)
    movie_frames = normal_values(own_keys[0], (PLANES, FRAMES, H, W), 1.0, 6.0, ((0, 2), (1, 4), (2, 2)))
    pixel_mask = place_ends((jax.random.randint(key_list[1], (H, W), 0, 4) < 3).astype(jnp.int32), jax.random.fold_in(key_list[1], 1), 0, 1)
    tile_owner_keys = jax.random.split(jax.random.fold_in(key_list[2], 1), H // HH)
    tile_owner_turns = jax.random.permutation(jax.random.fold_in(key_list[2], 3), H // HH)
    tile_owner = jax.vmap(lambda own, number: deal_out(jax.random.fold_in(key_list[2], 2), own, number, HH, CLUSTERS, 1, CAP, 2))(tile_owner_keys, tile_owner_turns).reshape((H, 1))
    support = place_ends(jax.random.randint(key_list[3], (H, FP), 0, NCOMP), jax.random.fold_in(key_list[3], 1), 0, NCOMP - 1).astype(jnp.int32)
    templates = normal_values(key_list[4], (NCOMP, PLANES, W), (PLANES * W) ** -0.5, 0.25, ((1, 2),))
    row_taps = normal_values(key_list[5], (TAPS_S,), TAPS_S ** -0.5, 1.25, (), jnp.float32)
    col_taps = normal_values(key_list[6], (TAPS_S,), TAPS_S ** -0.5, 1.25, (), jnp.float32)
    lag_gains = normal_values(key_list[7], (CLUSTERS, BANDS, TAPS_T), (BANDS * TAPS_T) ** -0.5, 0.4375, ((0, 4),), jnp.float32)
    dilations = place_ends(jax.random.randint(key_list[8], (CLUSTERS, BANDS), 1, DMAX + 1), jax.random.fold_in(key_list[8], 1), 1, DMAX).astype(jnp.int32)
    return {"movie_frames": movie_frames, "pixel_mask": pixel_mask, "tile_owner": tile_owner, "support": support, "templates": templates, "row_taps": row_taps, "col_taps": col_taps, "lag_gains": lag_gains, "dilations": dilations}


def band_matrix(tap_values, rows_in, rows_out, sign, offset):
    inner_idx = jnp.arange(rows_in, dtype=jnp.int32)[:, None]
    outer_idx = jnp.arange(rows_out, dtype=jnp.int32)[None, :]
    where_tap = sign * (inner_idx - outer_idx) + offset
    tap_index = jnp.arange(tap_values.shape[0], dtype=jnp.int32)
    picked_taps = where_tap[:, :, None] == tap_index[None, None, :]
    weights = jnp.where(picked_taps, tap_values[None, None, :], jnp.zeros((), tap_values.dtype))
    return jnp.sum(weights, axis=2).astype(jnp.bfloat16)


def lag_matrix(cluster_gains, cluster_lags, frame_count):
    tap_count = cluster_gains.shape[1]
    half_taps = (tap_count - 1) // 2
    lag_values = jnp.arange(2 * frame_count - 1, dtype=jnp.int32) - (frame_count - 1)
    tap_offsets = jnp.arange(tap_count, dtype=jnp.int32) - half_taps
    lag_hits = lag_values[None, :, None] == cluster_lags[:, None, None] * tap_offsets[None, None, :]
    spread = jnp.where(lag_hits, cluster_gains[:, None, :], jnp.zeros((), cluster_gains.dtype))
    kernel = jnp.sum(spread, axis=(0, 2))
    flipped = jnp.concatenate([kernel[::-1], jnp.zeros((1,), kernel.dtype)])
    tiled = jnp.broadcast_to(flipped, (frame_count, 2 * frame_count)).reshape(-1)
    tiled = tiled[: frame_count * (2 * frame_count - 1)].reshape(frame_count, 2 * frame_count - 1)
    return tiled[:, frame_count - 1:].astype(jnp.bfloat16)


def slot_table(owners, cluster_count, capacity):
    row_count = owners.shape[0]
    owner_marks = (owners[:, None] == jnp.arange(cluster_count, dtype=jnp.int32)[None, :]).astype(jnp.int32)
    before = jnp.cumsum(owner_marks, axis=0) - owner_marks
    slot_ranks = jnp.sum(before * owner_marks, axis=1)
    slot_of = owners * capacity + slot_ranks
    places = jnp.arange(cluster_count * capacity, dtype=jnp.int32)
    chosen = (slot_of[None, :] == places[:, None]).astype(jnp.int32)
    sources = jnp.sum(chosen * jnp.arange(row_count, dtype=jnp.int32)[None, :], axis=1)
    return slot_of, sources


def reference(movie_frames, pixel_mask, tile_owner, support, templates, row_taps, col_taps, lag_gains, dilations):
    plane_count, frame_count, row_count, col_count = movie_frames.shape
    half_rows = row_count // N_REP
    rim_width = (row_taps.shape[0] - 1) // 2
    col_fwd = band_matrix(col_taps, col_count, col_count, 1, rim_width)
    row_fwd = band_matrix(row_taps, row_count, row_count, 1, rim_width)
    col_adj = band_matrix(col_taps, col_count, col_count, -1, rim_width)
    row_adj = band_matrix(row_taps, row_count, row_count, -1, rim_width)
    mask_value = pixel_mask.astype(jnp.float32)

    def forward_plane(plane_frames):
        smooth = jnp.dot(plane_frames, col_fwd, preferred_element_type=jnp.float32).astype(jnp.bfloat16)
        along = jnp.einsum('thw,hg->tgw', smooth.astype(jnp.float32), row_fwd.astype(jnp.float32), precision=lax.Precision.HIGHEST)
        return (along * mask_value[None]).astype(jnp.bfloat16)

    filtered = lax.map(forward_plane, movie_frames)

    owner_halves = tile_owner[:, 0].reshape(N_REP, half_rows)
    slot_parts = []
    source_parts = []
    for half_index in range(N_REP):
        slot_of, sources = slot_table(owner_halves[half_index], CLUSTERS, CAP)
        slot_parts.append(slot_of)
        source_parts.append(sources + half_index * half_rows)
    picked_all = jnp.stack(source_parts).reshape(N_REP, CLUSTERS, CAP)
    picked_all = jnp.transpose(picked_all, (1, 0, 2)).reshape(CLUSTERS, N_REP * CAP).astype(jnp.int32)

    def per_cluster(inputs):
        cluster_gains, cluster_lags, picked = inputs
        lag_table = lag_matrix(cluster_gains, cluster_lags, frame_count)
        columns = jnp.take(filtered, picked, axis=2)
        mixed_cols = jnp.einsum('pscw,st->ptcw', columns.astype(jnp.float32), lag_table.astype(jnp.float32), precision=lax.Precision.HIGHEST).astype(jnp.bfloat16)
        shapes = jnp.take(templates, jnp.take(support, picked, axis=0), axis=0)
        scores = jnp.einsum('cjpw,ptcw->cjt', shapes.astype(jnp.float32), mixed_cols.astype(jnp.float32), precision=lax.Precision.HIGHEST)
        return jnp.maximum(scores, 0.0).astype(jnp.bfloat16)

    cluster_traces = lax.map(per_cluster, (lag_gains, dilations, picked_all))
    foot_count = cluster_traces.shape[2]
    flat_parts = []
    for half_index in range(N_REP):
        owners_here = owner_halves[half_index]
        slot_ranks = slot_parts[half_index] - owners_here * CAP
        flat_parts.append(owners_here * (N_REP * CAP) + half_index * CAP + slot_ranks)
    flat_index = jnp.concatenate(flat_parts).astype(jnp.int32)
    flat_traces = cluster_traces.reshape(CLUSTERS * N_REP * CAP, foot_count, frame_count)
    tile_traces = jnp.take(flat_traces, flat_index, axis=0)

    tile_shapes = jnp.take(templates, support, axis=0)
    plane_shapes = jnp.transpose(tile_shapes, (2, 0, 1, 3))
    trace_value = tile_traces.astype(jnp.float32)

    def backward_plane(inputs):
        plane_filtered, shape_plane = inputs
        model_part = jnp.einsum('hjw,hjt->thw', shape_plane.astype(jnp.float32), trace_value, precision=lax.Precision.HIGHEST)
        residual = (plane_filtered.astype(jnp.float32) - mask_value[None] * model_part).astype(jnp.bfloat16)
        back_rows = jnp.einsum('thw,hg->tgw', residual.astype(jnp.float32), row_adj.astype(jnp.float32), precision=lax.Precision.HIGHEST).astype(jnp.bfloat16)
        return jnp.dot(back_rows, col_adj, preferred_element_type=jnp.float32).astype(jnp.bfloat16)

    back_projected = lax.map(backward_plane, (filtered, plane_shapes))
    traces = jnp.transpose(tile_traces, (1, 2, 0))
    return traces, back_projected
```

```python
import functools

import jax
import jax.numpy as jnp
from jax import lax
from jax.experimental import pallas as pl
from jax.experimental.pallas import tpu as pltpu
from jax.sharding import PartitionSpec as P

MESH = pl.DeviceIdType.MESH
BF = jnp.bfloat16
F32 = jnp.float32


def extended(cells, axis, dim, width):
    count = lax.axis_size(axis)
    ends = count - 1
    head = lax.slice_in_dim(cells, 0, width, axis=dim)
    tail = lax.slice_in_dim(cells, cells.shape[dim] - width, cells.shape[dim], axis=dim)
    return jnp.concatenate(
        [
            lax.ppermute(tail, axis, [(i, (i + 1) % count) for i in range(ends)]),
            cells,
            lax.ppermute(head, axis, [((i + 1) % count, i) for i in range(ends)]),
        ],
        axis=dim,
    )


def band_matrix(tap_values, rows_in, rows_out, sign, offset):
    inner_idx = jnp.arange(rows_in, dtype=jnp.int32)[:, None]
    outer_idx = jnp.arange(rows_out, dtype=jnp.int32)[None, :]
    where_tap = sign * (inner_idx - outer_idx) + offset
    tap_index = jnp.arange(tap_values.shape[0], dtype=jnp.int32)
    picked_taps = where_tap[:, :, None] == tap_index[None, None, :]
    weights = jnp.where(picked_taps, tap_values[None, None, :], jnp.zeros((), tap_values.dtype))
    return jnp.sum(weights, axis=2).astype(BF)


def lag_matrix(cluster_gains, cluster_lags, frame_count):
    tap_count = cluster_gains.shape[1]
    half_taps = (tap_count - 1) // 2
    lag_values = jnp.arange(2 * frame_count - 1, dtype=jnp.int32) - (frame_count - 1)
    tap_offsets = jnp.arange(tap_count, dtype=jnp.int32) - half_taps
    lag_hits = lag_values[None, :, None] == cluster_lags[:, None, None] * tap_offsets[None, None, :]
    spread = jnp.where(lag_hits, cluster_gains[:, None, :], jnp.zeros((), cluster_gains.dtype))
    kernel = jnp.sum(spread, axis=(0, 2))
    padded = jnp.concatenate([kernel, jnp.zeros((1,), kernel.dtype)])
    tiled = jnp.broadcast_to(padded, (frame_count, 2 * frame_count)).reshape(-1)
    tiled = tiled[: frame_count * (2 * frame_count - 1)].reshape(frame_count, 2 * frame_count - 1)
    return tiled[:, frame_count - 1 :].astype(BF)


def mid_kernel(
    f_ref, sup_ref, own_ref, temp_ref, lag_ref, mask_ref,
    res_ref, tr_ref,
    hot, pall, part, xrecv, zsend, gath, lag_all, tbuf, tr_all, fold,
    lag_s, lag_r, x1_s, x1_r, z1_s, z1_r, z2_s, z2_r, x2_s, x2_r,
):
    np_ = lax.axis_size("planes")
    nw = lax.axis_size("wide")
    p = lax.axis_index("planes")
    z = lax.axis_index("wide")
    blocks, hb, frames, comps = part.shape
    shapes = temp_ref.shape[0]
    tile = min(256, shapes)
    total = nw * frames

    barrier = pltpu.get_barrier_semaphore()
    for k in range(1, nw):
        pl.semaphore_signal(barrier, inc=1, device_id={"wide": lax.rem(z + k, nw)}, device_id_type=MESH)
    for k in range(1, np_):
        pl.semaphore_signal(barrier, inc=1, device_id={"planes": lax.rem(p + k, np_)}, device_id_type=MESH)
    pl.semaphore_wait(barrier, nw - 1 + np_ - 1)

    def to_wide(src, dst, send, recv, k):
        return pltpu.make_async_remote_copy(
            src_ref=src, dst_ref=dst, send_sem=send.at[k - 1], recv_sem=recv.at[k - 1],
            device_id={"wide": lax.rem(z + k, nw)}, device_id_type=MESH)

    def to_plane(src, dst, send, recv, dp, zi):
        slot = (dp - 1) * nw + zi
        return pltpu.make_async_remote_copy(
            src_ref=src, dst_ref=dst, send_sem=send.at[slot], recv_sem=recv.at[slot],
            device_id={"planes": lax.rem(p + dp, np_)}, device_id_type=MESH)

    def lag_copy(k):
        return to_wide(lag_ref, lag_all.at[z], lag_s, lag_r, k)

    def x1_copy(dp, zi):
        return to_plane(part.at[lax.rem(p + dp, np_) * nw + zi], xrecv.at[(dp - 1) * nw + zi], x1_s, x1_r, dp, zi)

    def z1_copy(k):
        return to_wide(zsend.at[lax.rem(z + k, nw)], gath.at[z], z1_s, z1_r, k)

    def z2_copy(k):
        return to_wide(tbuf.at[lax.rem(z + k, nw)], tr_all.at[p * nw + z], z2_s, z2_r, k)

    def x2_copy(dp, zi):
        return to_plane(tr_all.at[p * nw + zi], tr_all.at[p * nw + zi], x2_s, x2_r, dp, zi)

    for k in range(1, nw):
        lag_copy(k).start()
    lag_all[z] = lag_ref[...]

    ids = lax.broadcasted_iota(jnp.int32, (tile, comps), 0)

    def project(b):
        base = b * hb
        f_blk = f_ref[pl.ds(base, hb)].reshape(hb * frames, f_ref.shape[2])
        pall[...] = lax.dot_general(
            f_blk, temp_ref[...], (((1,), (1,)), ((), ())), preferred_element_type=F32).astype(BF)
        sup = sup_ref[b]
        for i in range(hb):
            row = sup[i : i + 1, :]
            for q in range(0, shapes, tile):
                hot[base + i, q : q + tile, :] = jnp.where(ids == row - q, 1.0, 0.0).astype(BF)
            part[b, i] = jnp.dot(
                pall[i * frames : (i + 1) * frames, :], hot[base + i], preferred_element_type=F32).astype(BF)

    def others(n, carry):
        dp = n // nw + 1
        zi = lax.rem(z + 1 + n, nw)
        project(lax.rem(p + dp, np_) * nw + zi)
        x1_copy(dp, zi).start()
        return carry

    lax.fori_loop(0, (np_ - 1) * nw, others, 0)

    def mine(n, carry):
        zi = lax.rem(z + 1 + n, nw)
        b = p * nw + zi
        project(b)
        acc = part[b].astype(F32)
        for dp in range(1, np_):
            x1_copy(dp, zi).wait_recv()
            acc = acc + xrecv[(dp - 1) * nw + zi].astype(F32)
        zsend[zi] = acc.astype(BF)

        @pl.when(n < nw - 1)
        def _():
            z1_copy(n + 1).start()

        return carry

    lax.fori_loop(0, nw, mine, 0)
    gath[z] = zsend[z]

    def arrived(k, carry):
        lag_copy(k).wait()
        z1_copy(k).wait()
        return carry

    lax.fori_loop(1, nw, arrived, 0)

    me = p * nw + z
    for i in range(hb):
        table = lag_all[own_ref[me * hb + i]]
        columns = gath[:, i].reshape(total, comps)
        scores = jnp.dot(table, columns, preferred_element_type=F32)
        tbuf[:, i] = jnp.maximum(scores, 0.0).astype(BF).reshape(nw, frames, comps)

    def give(k, carry):
        z2_copy(k).start()
        return carry

    lax.fori_loop(1, nw, give, 0)
    tr_all[me] = tbuf[z]

    def model(b):
        base = b * hb
        for i in range(hb):
            fold[i * frames : (i + 1) * frames, :] = lax.dot_general(
                tr_all[b, i], hot[base + i], (((1,), (1,)), ((), ())), preferred_element_type=F32).astype(BF)
        out = jnp.dot(fold[...], temp_ref[...], preferred_element_type=F32)
        out = out.reshape(hb, frames, out.shape[1])
        mask = mask_ref[pl.ds(base, hb)]
        res_ref[pl.ds(base, hb)] = (f_ref[pl.ds(base, hb)].astype(F32) - mask * out).astype(BF)

    def same_plane(k, carry):
        zi = lax.rem(z + nw - k, nw)

        @pl.when(k > 0)
        def _():
            z2_copy(lax.max(k, 1)).wait_recv()

        for dp in range(1, np_):
            x2_copy(dp, zi).start()
        model(p * nw + zi)
        return carry

    lax.fori_loop(0, nw, same_plane, 0)

    def other_planes(n, carry):
        dp = n // nw + 1
        zi = lax.rem(z + nw - lax.rem(n, nw), nw)
        x2_copy(dp, zi).wait_recv()
        model(lax.rem(p + np_ - dp, np_) * nw + zi)
        return carry

    lax.fori_loop(0, (np_ - 1) * nw, other_planes, 0)
    tr_ref[...] = tr_all[...]

    def drained_planes(n, carry):
        x1_copy(n // nw + 1, lax.rem(n, nw)).wait_send()
        x2_copy(n // nw + 1, lax.rem(n, nw)).wait_send()
        return carry

    lax.fori_loop(0, (np_ - 1) * nw, drained_planes, 0)

    def drained_wide(k, carry):
        z2_copy(k).wait_send()
        return carry

    lax.fori_loop(1, nw, drained_wide, 0)


def middle(filtered, support, owners, shapes, lag_table, mask):
    np_ = lax.axis_size("planes")
    nw = lax.axis_size("wide")
    blocks = np_ * nw
    rows, frames, pixels = filtered.shape
    hb = rows // blocks
    comps = support.shape[1]
    count = shapes.shape[0]
    total = nw * frames
    vm = pl.BlockSpec(memory_space=pltpu.VMEM)
    dma = pltpu.SemaphoreType.DMA
    piece = (hb, frames, comps)
    res, tr = pl.pallas_call(
        mid_kernel,
        out_shape=(
            jax.ShapeDtypeStruct(filtered.shape, BF),
            jax.ShapeDtypeStruct((blocks,) + piece, BF),
        ),
        in_specs=[vm, vm, pl.BlockSpec(memory_space=pltpu.SMEM), vm, vm, vm],
        out_specs=(vm, vm),
        scratch_shapes=[
            pltpu.VMEM((rows, count, comps), BF),
            pltpu.VMEM((hb * frames, count), BF),
            pltpu.VMEM((blocks,) + piece, BF),
            pltpu.VMEM(((np_ - 1) * nw,) + piece, BF),
            pltpu.VMEM((nw,) + piece, BF),
            pltpu.VMEM((nw,) + piece, BF),
            pltpu.VMEM((nw, total, total), BF),
            pltpu.VMEM((nw,) + piece, BF),
            pltpu.VMEM((blocks,) + piece, BF),
            pltpu.VMEM((hb * frames, count), BF),
            dma((nw - 1,)), dma((nw - 1,)),
            dma(((np_ - 1) * nw,)), dma(((np_ - 1) * nw,)),
            dma((nw - 1,)), dma((nw - 1,)),
            dma((nw - 1,)), dma((nw - 1,)),
            dma(((np_ - 1) * nw,)), dma(((np_ - 1) * nw,)),
        ],
        compiler_params=pltpu.CompilerParams(
            collective_id=0, has_side_effects=True, vmem_limit_bytes=60 * 1024 * 1024
        ),
    )(filtered, support.reshape(blocks, hb, comps), owners, shapes, lag_table, mask)
    return res, tr.reshape(rows, frames, comps)


def on_device(
    movie_frames, pixel_mask, tile_owner, support, templates, row_taps, col_taps, lag_gains, dilations
):
    planes_here, frames_here, rows_here, col_count = movie_frames.shape
    nw = lax.axis_size("wide")
    rim = (row_taps.shape[0] - 1) // 2
    mask_value = pixel_mask.astype(F32)
    col_fwd = band_matrix(col_taps, col_count, col_count, 1, rim)
    smooth = jnp.dot(movie_frames, col_fwd, preferred_element_type=F32).astype(BF)
    padded = extended(smooth, "rep", 2, rim)
    row_fwd = band_matrix(row_taps, rows_here + 2 * rim, rows_here, 1, 0)
    along = jnp.einsum("pfew,eh->hfpw", padded, row_fwd, preferred_element_type=F32)
    filtered = (along * mask_value[:, None, None, :]).astype(BF)
    filtered = filtered.reshape(rows_here, frames_here, planes_here * col_count)
    lag_table = lag_matrix(lag_gains[0], dilations[0], frames_here * nw)
    wide_mask = jnp.tile(mask_value, (1, planes_here))[:, None, :]
    shapes = templates.reshape(templates.shape[0], planes_here * col_count)
    residual, traces = middle(filtered, support, tile_owner[:, 0], shapes, lag_table, wide_mask)

    padded_back = extended(residual, "rep", 0, rim)
    padded_back = padded_back.reshape(rows_here + 2 * rim, frames_here, planes_here, col_count)
    row_adj = band_matrix(row_taps, rows_here + 2 * rim, rows_here, -1, 2 * rim)
    back_rows = jnp.einsum("efpw,eh->pfhw", padded_back, row_adj, preferred_element_type=F32).astype(BF)
    col_adj = band_matrix(col_taps, col_count, col_count, -1, rim)
    back_projected = jnp.dot(back_rows, col_adj, preferred_element_type=F32).astype(BF)

    share = traces.shape[2] // lax.axis_size("planes")
    mine = lax.dynamic_slice_in_dim(traces, lax.axis_index("planes") * share, share, 2)
    return (jnp.transpose(mine, (2, 1, 0)), back_projected)


def solution(mesh):
    return jax.shard_map(
        on_device,
        mesh=mesh,
        in_specs=(
            P("planes", ("groups", "wide"), "rep", None),
            P("rep", None),
            P("rep", None),
            P("rep", None),
            P(None, "planes", None),
            P(),
            P(),
            P("wide", None, None),
            P("wide", None),
        ),
        out_specs=(
            P("planes", ("groups", "wide"), "rep"),
            P("planes", ("groups", "wide"), "rep", None),
        ),
        check_vma=False,
    )
```

```python
import functools

import jax
import jax.numpy as jnp
from jax import lax
from jax.experimental import pallas as pl
from jax.experimental.pallas import tpu as pltpu
from jax.sharding import PartitionSpec as P

MESH = pl.DeviceIdType.MESH
BF = jnp.bfloat16
F32 = jnp.float32


def banded(taps_ref, where_tap):
    out = jnp.zeros(where_tap.shape, F32)
    for k in range(taps_ref.shape[0]):
        out = jnp.where(where_tap == k, taps_ref[k], out)
    return out.astype(BF)


def lag_table(gain_ref, dil_ref, total):
    bands, taps = gain_ref.shape[1:]
    lag = lax.broadcasted_iota(jnp.int32, (1, 2 * total), 1) - (total - 1)
    row = jnp.zeros((1, 2 * total), F32)
    for b in range(bands):
        for k in range(taps):
            row = row + jnp.where(lag == dil_ref[0, b] * (k - (taps - 1) // 2), gain_ref[0, b, k], 0.0)
    spread = jnp.broadcast_to(row, (total, 2 * total))
    return pltpu.roll(spread, total + 1, 1, stride=1, stride_axis=0)[:, :total].astype(BF)


def kernel(
    movie_ref, sup_ref, own_ref, temp_ref, gain_ref, dil_ref, mask_ref, row_ref, col_ref,
    back_ref, tr_ref,
    hot, pall, part, xrecv, zsend, gath, lag_ref, lag_all, tbuf, tr_all, fold,
    spad, top_in, bot_in, top_res, bot_res, cells, tr_rows, tr_out,
    lag_s, lag_r, x1_s, x1_r, z1_s, z1_r, z2_s, z2_r, x2_s, x2_r, h_s, h_r,
):
    np_ = lax.axis_size("planes")
    nw = lax.axis_size("wide")
    nr = lax.axis_size("rep")
    p = lax.axis_index("planes")
    z = lax.axis_index("wide")
    r = lax.axis_index("rep")
    blocks, hb, frames, comps = part.shape
    planes_here, _, rows, width = movie_ref.shape
    rim = (row_ref.shape[0] - 1) // 2
    edge = (spad.shape[2] - rows) // 2
    images = planes_here * frames
    shapes = temp_ref.shape[0]
    tile = min(256, shapes)
    total = nw * frames
    step = 4

    barrier = pltpu.get_barrier_semaphore()

    @pl.when(r > 0)
    def _():
        pl.semaphore_signal(barrier, inc=1, device_id={"rep": r - 1}, device_id_type=MESH)

    @pl.when(r < nr - 1)
    def _():
        pl.semaphore_signal(barrier, inc=1, device_id={"rep": r + 1}, device_id_type=MESH)

    for k in range(1, nw):
        pl.semaphore_signal(barrier, inc=1, device_id={"wide": lax.rem(z + k, nw)}, device_id_type=MESH)
    for k in range(1, np_):
        pl.semaphore_signal(barrier, inc=1, device_id={"planes": lax.rem(p + k, np_)}, device_id_type=MESH)

    lag_ref[...] = lag_table(gain_ref, dil_ref, total)
    lag_all[z] = lag_ref[...]
    inner = lax.broadcasted_iota(jnp.int32, (width, width), 0)
    outer = lax.broadcasted_iota(jnp.int32, (width, width), 1)
    col_fwd = banded(col_ref, inner - outer + rim)

    pl.semaphore_wait(barrier, nw - 1 + np_ - 1 + lax.min(r, 1) + lax.min(nr - 1 - r, 1))

    def halo(source, lo, hi, top, bot, base):
        down = pltpu.make_async_remote_copy(
            src_ref=source.at[:, :, hi : hi + edge], dst_ref=top,
            send_sem=h_s.at[base], recv_sem=h_r.at[base],
            device_id={"rep": lax.min(r + 1, nr - 1)}, device_id_type=MESH)
        up = pltpu.make_async_remote_copy(
            src_ref=source.at[:, :, lo : lo + edge], dst_ref=bot,
            send_sem=h_s.at[base + 1], recv_sem=h_r.at[base + 1],
            device_id={"rep": lax.max(r - 1, 0)}, device_id_type=MESH)
        return down, up

    def halo_start(copies):
        @pl.when(r < nr - 1)
        def _():
            copies[0].start()

        @pl.when(r > 0)
        def _():
            copies[1].start()

    def halo_finish(copies, top, bot):
        @pl.when(r > 0)
        def _():
            copies[0].wait_recv()
            copies[1].wait_send()

        @pl.when(r == 0)
        def _():
            top[...] = jnp.zeros_like(top)

        @pl.when(r < nr - 1)
        def _():
            copies[1].wait_recv()
            copies[0].wait_send()

        @pl.when(r == nr - 1)
        def _():
            bot[...] = jnp.zeros_like(bot)

    in_copies = halo(movie_ref, 0, rows - edge, top_in, bot_in, 0)
    halo_start(in_copies)

    def to_wide(src, dst, send, recv, k):
        return pltpu.make_async_remote_copy(
            src_ref=src, dst_ref=dst, send_sem=send.at[k - 1], recv_sem=recv.at[k - 1],
            device_id={"wide": lax.rem(z + k, nw)}, device_id_type=MESH)

    def to_plane(src, dst, send, recv, dp, zi):
        slot = (dp - 1) * nw + zi
        return pltpu.make_async_remote_copy(
            src_ref=src, dst_ref=dst, send_sem=send.at[slot], recv_sem=recv.at[slot],
            device_id={"planes": lax.rem(p + dp, np_)}, device_id_type=MESH)

    def lag_copy(k):
        return to_wide(lag_ref, lag_all.at[z], lag_s, lag_r, k)

    def x1_copy(dp, zi):
        return to_plane(part.at[lax.rem(p + dp, np_) * nw + zi], xrecv.at[(dp - 1) * nw + zi], x1_s, x1_r, dp, zi)

    def z1_copy(k):
        return to_wide(zsend.at[lax.rem(z + k, nw)], gath.at[z], z1_s, z1_r, k)

    def z2_copy(k):
        return to_wide(tbuf.at[lax.rem(z + k, nw)], tr_all.at[p * nw + z], z2_s, z2_r, k)

    def x2_copy(dp, zi):
        return to_plane(tr_all.at[p * nw + zi], tr_all.at[p * nw + zi], x2_s, x2_r, dp, zi)

    for k in range(1, nw):
        lag_copy(k).start()

    def smooth(n, carry):
        for u in range(step):
            q = n * step + u
            pi, f = q // frames, lax.rem(q, frames)
            spad[pi, f, edge : edge + rows] = jnp.dot(
                movie_ref[pi, f], col_fwd, preferred_element_type=F32).astype(BF)
        return carry

    lax.fori_loop(0, images // step, smooth, 0)
    here = lax.broadcasted_iota(jnp.int32, (rows, rows + 2 * edge), 0)
    there = lax.broadcasted_iota(jnp.int32, (rows, rows + 2 * edge), 1) - edge
    row_fwd = banded(row_ref, there - here + rim)
    halo_finish(in_copies, top_in, bot_in)
    for pi in range(planes_here):
        for held, at in ((top_in, 0), (bot_in, edge + rows)):
            spad[pi, :, at : at + edge] = jnp.dot(
                held[pi].reshape(frames * edge, width), col_fwd, preferred_element_type=F32
            ).astype(BF).reshape(frames, edge, width)
    mask_all = mask_ref[...].reshape(rows, width).astype(F32)

    def along(n, carry):
        for u in range(step):
            q = n * step + u
            pi, f = q // frames, lax.rem(q, frames)
            value = jnp.dot(row_fwd, spad[pi, f], preferred_element_type=F32) * mask_all
            cells[pi, pl.ds(f, rows, stride=frames), :] = value
        return carry

    lax.fori_loop(0, images // step, along, 0)

    def block_cells(b):
        span = pl.ds(b * hb * frames, hb * frames)
        return jnp.concatenate([cells[pi, span, :] for pi in range(planes_here)], axis=1).astype(BF)

    ids = lax.broadcasted_iota(jnp.int32, (tile, comps), 0)

    def project(b):
        base = b * hb
        f_blk = block_cells(b)
        pall[...] = lax.dot_general(
            f_blk, temp_ref[...], (((1,), (1,)), ((), ())), preferred_element_type=F32).astype(BF)
        sup = sup_ref[b]
        for i in range(hb):
            row = sup[i : i + 1, :]
            for q in range(0, shapes, tile):
                hot[base + i, q : q + tile, :] = jnp.where(ids == row - q, 1.0, 0.0).astype(BF)
            part[b, i] = jnp.dot(
                pall[i * frames : (i + 1) * frames, :], hot[base + i], preferred_element_type=F32).astype(BF)

    def others(n, carry):
        dp = n // nw + 1
        zi = lax.rem(z + 1 + n, nw)
        project(lax.rem(p + dp, np_) * nw + zi)
        x1_copy(dp, zi).start()
        return carry

    lax.fori_loop(0, (np_ - 1) * nw, others, 0)

    def mine(n, carry):
        zi = lax.rem(z + 1 + n, nw)
        b = p * nw + zi
        project(b)
        acc = part[b].astype(F32)
        for dp in range(1, np_):
            x1_copy(dp, zi).wait_recv()
            acc = acc + xrecv[(dp - 1) * nw + zi].astype(F32)
        zsend[zi] = acc.astype(BF)

        @pl.when(n < nw - 1)
        def _():
            z1_copy(n + 1).start()

        return carry

    lax.fori_loop(0, nw, mine, 0)
    gath[z] = zsend[z]

    def arrived(k, carry):
        lag_copy(k).wait()
        z1_copy(k).wait()
        return carry

    lax.fori_loop(1, nw, arrived, 0)

    me = p * nw + z
    for i in range(hb):
        table = lag_all[own_ref[me * hb + i]]
        columns = gath[:, i].reshape(total, comps)
        scores = jnp.dot(table, columns, preferred_element_type=F32)
        tbuf[:, i] = jnp.maximum(scores, 0.0).astype(BF).reshape(nw, frames, comps)

    def give(k, carry):
        z2_copy(k).start()
        return carry

    lax.fori_loop(1, nw, give, 0)
    tr_all[me] = tbuf[z]

    def model(b):
        base = b * hb
        for i in range(hb):
            fold[i * frames : (i + 1) * frames, :] = lax.dot_general(
                tr_all[b, i], hot[base + i], (((1,), (1,)), ((), ())), preferred_element_type=F32).astype(BF)
        tr_rows[pl.ds(base * frames, hb * frames), :] = tr_all[b].reshape(hb * frames, comps).astype(F32)
        out = jnp.dot(fold[...], temp_ref[...], preferred_element_type=F32)
        mask = mask_ref[b].astype(F32)
        mask = jnp.broadcast_to(mask[:, None, :], (hb, frames, width)).reshape(hb * frames, width)
        mask = jnp.concatenate([mask] * planes_here, axis=1)
        left = (block_cells(b).astype(F32) - mask * out).astype(BF).astype(F32)
        for pi in range(planes_here):
            cells[pi, pl.ds(base * frames, hb * frames), :] = left[:, pi * width : (pi + 1) * width]

    def same_plane(k, carry):
        zi = lax.rem(z + nw - k, nw)

        @pl.when(k > 0)
        def _():
            z2_copy(lax.max(k, 1)).wait_recv()

        for dp in range(1, np_):
            x2_copy(dp, zi).start()
        model(p * nw + zi)
        return carry

    lax.fori_loop(0, nw, same_plane, 0)

    def other_planes(n, carry):
        dp = n // nw + 1
        zi = lax.rem(z + nw - lax.rem(n, nw), nw)
        x2_copy(dp, zi).wait_recv()
        model(lax.rem(p + np_ - dp, np_) * nw + zi)
        return carry

    lax.fori_loop(0, (np_ - 1) * nw, other_planes, 0)

    def edges(n, carry):
        for u in range(step):
            q = n * step + u
            pi, f = q // frames, lax.rem(q, frames)
            for at in (0, rows - edge):
                spad[pi, f, edge + at : 2 * edge + at] = cells[
                    pi, pl.ds(f + at * frames, edge, stride=frames), :].astype(BF)
        return carry

    lax.fori_loop(0, images // step, edges, 0)
    out_copies = halo(spad, edge, rows, top_res, bot_res, 2)
    halo_start(out_copies)

    def inside(n, carry):
        for u in range(step):
            q = n * step + u
            pi, f = q // frames, lax.rem(q, frames)
            spad[pi, f, 2 * edge : rows] = cells[
                pi, pl.ds(f + edge * frames, rows - 2 * edge, stride=frames), :].astype(BF)
        return carry

    lax.fori_loop(0, images // step, inside, 0)

    share = comps // np_
    pick = (
        lax.broadcasted_iota(jnp.int32, (share, comps), 0) + p * share
        == lax.broadcasted_iota(jnp.int32, (share, comps), 1)
    )
    pick = jnp.where(pick, 1.0, 0.0).astype(BF)
    for t in range(frames):
        one = tr_rows[pl.ds(t, rows, stride=frames), :].astype(BF)
        tr_out[pl.ds(t, share, stride=frames), :] = lax.dot_general(
            pick, one, (((1,), (1,)), ((), ())), preferred_element_type=F32)
    tr_ref[...] = tr_out[...].astype(BF).reshape(tr_ref.shape)

    row_adj = banded(row_ref, here - there + rim)
    col_adj = banded(col_ref, outer - inner + rim)
    halo_finish(out_copies, top_res, bot_res)
    spad[:, :, 0:edge] = top_res[...]
    spad[:, :, edge + rows :] = bot_res[...]

    def back(n, carry):
        for u in range(step):
            q = n * step + u
            pi, f = q // frames, lax.rem(q, frames)
            value = jnp.dot(row_adj, spad[pi, f], preferred_element_type=F32).astype(BF)
            back_ref[pi, f] = jnp.dot(value, col_adj, preferred_element_type=F32).astype(BF)
        return carry

    lax.fori_loop(0, images // step, back, 0)

    def drained_planes(n, carry):
        x1_copy(n // nw + 1, lax.rem(n, nw)).wait_send()
        x2_copy(n // nw + 1, lax.rem(n, nw)).wait_send()
        return carry

    lax.fori_loop(0, (np_ - 1) * nw, drained_planes, 0)

    def drained_wide(k, carry):
        z2_copy(k).wait_send()
        return carry

    lax.fori_loop(1, nw, drained_wide, 0)


def on_device(
    movie_frames, pixel_mask, tile_owner, support, templates, row_taps, col_taps, lag_gains, dilations
):
    np_ = lax.axis_size("planes")
    nw = lax.axis_size("wide")
    blocks = np_ * nw
    planes_here, frames, rows, width = movie_frames.shape
    hb = rows // blocks
    comps = support.shape[1]
    count = templates.shape[0]
    total = nw * frames
    rim = (row_taps.shape[0] - 1) // 2
    edge = -(-rim // 16) * 16
    shapes = templates.reshape(count, planes_here * width)
    vm = pl.BlockSpec(memory_space=pltpu.VMEM)
    sm = pl.BlockSpec(memory_space=pltpu.SMEM)
    dma = pltpu.SemaphoreType.DMA
    piece = (hb, frames, comps)
    across = (np_ - 1) * nw
    halo = pltpu.VMEM((planes_here, frames, edge, width), BF)
    back, traces = pl.pallas_call(
        kernel,
        out_shape=(
            jax.ShapeDtypeStruct(movie_frames.shape, BF),
            jax.ShapeDtypeStruct((comps // np_, frames, rows), BF),
        ),
        in_specs=[vm, vm, sm, vm, sm, sm, vm, sm, sm],
        out_specs=(vm, vm),
        scratch_shapes=[
            pltpu.VMEM((rows, count, comps), BF),
            pltpu.VMEM((hb * frames, count), BF),
            pltpu.VMEM((blocks,) + piece, BF),
            pltpu.VMEM((across,) + piece, BF),
            pltpu.VMEM((nw,) + piece, BF),
            pltpu.VMEM((nw,) + piece, BF),
            pltpu.VMEM((total, total), BF),
            pltpu.VMEM((nw, total, total), BF),
            pltpu.VMEM((nw,) + piece, BF),
            pltpu.VMEM((blocks,) + piece, BF),
            pltpu.VMEM((hb * frames, count), BF),
            pltpu.VMEM((planes_here, frames, rows + 2 * edge, width), BF),
            halo, halo, halo, halo,
            pltpu.VMEM((planes_here, rows * frames, width), F32),
            pltpu.VMEM((rows * frames, comps), F32),
            pltpu.VMEM((comps // np_ * frames, rows), F32),
            dma((nw - 1,)), dma((nw - 1,)),
            dma((across,)), dma((across,)),
            dma((nw - 1,)), dma((nw - 1,)),
            dma((nw - 1,)), dma((nw - 1,)),
            dma((across,)), dma((across,)),
            dma((4,)), dma((4,)),
        ],
        compiler_params=pltpu.CompilerParams(
            collective_id=0, has_side_effects=True, vmem_limit_bytes=63 * 1024 * 1024
        ),
    )(
        movie_frames,
        support.reshape(blocks, hb, comps),
        tile_owner[:, 0],
        shapes,
        lag_gains,
        dilations,
        pixel_mask.reshape(blocks, hb, width),
        row_taps,
        col_taps,
    )
    return (traces, back)


def solution(mesh):
    return jax.shard_map(
        on_device,
        mesh=mesh,
        in_specs=(
            P("planes", ("groups", "wide"), "rep", None),
            P("rep", None),
            P("rep", None),
            P("rep", None),
            P(None, "planes", None),
            P(),
            P(),
            P("wide", None, None),
            P("wide", None),
        ),
        out_specs=(
            P("planes", ("groups", "wide"), "rep"),
            P("planes", ("groups", "wide"), "rep", None),
        ),
        check_vma=False,
    )
```

```python
import functools

import jax
import jax.numpy as jnp
from jax import lax
from jax.experimental import pallas as pl
from jax.experimental.pallas import tpu as pltpu
from jax.sharding import PartitionSpec as P

MESH = pl.DeviceIdType.MESH
BF = jnp.bfloat16
F32 = jnp.float32


def banded(taps_ref, where_tap):
    out = jnp.zeros(where_tap.shape, F32)
    for k in range(taps_ref.shape[0]):
        out = jnp.where(where_tap == k, taps_ref[k], out)
    return out.astype(BF)


def lag_table(gain_ref, dil_ref, total):
    bands, _, taps = gain_ref.shape
    lag = lax.broadcasted_iota(jnp.int32, (1, 2 * total), 1) - (total - 1)
    row = jnp.zeros((1, 2 * total), F32)
    for b in range(bands):
        for k in range(taps):
            row = row + jnp.where(lag == dil_ref[0, b] * (k - (taps - 1) // 2), gain_ref[b, 0, k], 0.0)
    spread = jnp.broadcast_to(row, (total, 2 * total))
    return pltpu.roll(spread, total + 1, 1, stride=1, stride_axis=0)[:, :total].astype(BF)


def kernel(
    movie_ref, sup_ref, own_ref, table_ref, gain_ref, dil_ref, mask_ref, row_ref, col_ref,
    spad, tr_ref,
    temp_ref, hot, pall, part, xrecv, zsend, gath, lag_ref, lag_all, tbuf, tr_all, fold,
    top_in, bot_in, top_res, bot_res, cells, tr_rows, tr_out,
    lag_s, lag_r, x1_s, x1_r, z1_s, z1_r, z2_s, z2_r, x2_s, x2_r, h_s, h_r,
):
    np_ = lax.axis_size("planes")
    nw = lax.axis_size("wide")
    nr = lax.axis_size("rep")
    p = lax.axis_index("planes")
    z = lax.axis_index("wide")
    r = lax.axis_index("rep")
    blocks, hb, frames, comps = part.shape
    planes_here, _, rows, width = movie_ref.shape
    rim = (row_ref.shape[0] - 1) // 2
    edge = (spad.shape[2] - rows) // 2
    images = planes_here * frames
    shapes = temp_ref.shape[0]
    tile = min(256, shapes)
    total = nw * frames
    step = 4

    barrier = pltpu.get_barrier_semaphore()

    @pl.when(r > 0)
    def _():
        pl.semaphore_signal(barrier, inc=1, device_id={"rep": r - 1}, device_id_type=MESH)

    @pl.when(r < nr - 1)
    def _():
        pl.semaphore_signal(barrier, inc=1, device_id={"rep": r + 1}, device_id_type=MESH)

    for k in range(1, nw):
        pl.semaphore_signal(barrier, inc=1, device_id={"wide": lax.rem(z + k, nw)}, device_id_type=MESH)
    for k in range(1, np_):
        pl.semaphore_signal(barrier, inc=1, device_id={"planes": lax.rem(p + k, np_)}, device_id_type=MESH)

    lag_ref[...] = lag_table(gain_ref, dil_ref, total)
    lag_all[z] = lag_ref[...]
    for pi in range(planes_here):
        temp_ref[:, pi * width : (pi + 1) * width] = table_ref[:, pi, :]
    inner = lax.broadcasted_iota(jnp.int32, (width, width), 0)
    outer = lax.broadcasted_iota(jnp.int32, (width, width), 1)
    col_fwd = banded(col_ref, inner - outer + rim)

    pl.semaphore_wait(barrier, nw - 1 + np_ - 1 + lax.min(r, 1) + lax.min(nr - 1 - r, 1))

    def halo(source, lo, hi, top, bot, base):
        down = pltpu.make_async_remote_copy(
            src_ref=source.at[:, :, hi : hi + edge], dst_ref=top,
            send_sem=h_s.at[base], recv_sem=h_r.at[base],
            device_id={"rep": lax.min(r + 1, nr - 1)}, device_id_type=MESH)
        up = pltpu.make_async_remote_copy(
            src_ref=source.at[:, :, lo : lo + edge], dst_ref=bot,
            send_sem=h_s.at[base + 1], recv_sem=h_r.at[base + 1],
            device_id={"rep": lax.max(r - 1, 0)}, device_id_type=MESH)
        return down, up

    def halo_start(copies):
        @pl.when(r < nr - 1)
        def _():
            copies[0].start()

        @pl.when(r > 0)
        def _():
            copies[1].start()

    def halo_finish(copies, top, bot):
        @pl.when(r > 0)
        def _():
            copies[0].wait_recv()
            copies[1].wait_send()

        @pl.when(r == 0)
        def _():
            top[...] = jnp.zeros_like(top)

        @pl.when(r < nr - 1)
        def _():
            copies[1].wait_recv()
            copies[0].wait_send()

        @pl.when(r == nr - 1)
        def _():
            bot[...] = jnp.zeros_like(bot)

    in_copies = halo(movie_ref, 0, rows - edge, top_in, bot_in, 0)
    halo_start(in_copies)

    def to_wide(src, dst, send, recv, k):
        return pltpu.make_async_remote_copy(
            src_ref=src, dst_ref=dst, send_sem=send.at[k - 1], recv_sem=recv.at[k - 1],
            device_id={"wide": lax.rem(z + k, nw)}, device_id_type=MESH)

    def to_plane(src, dst, send, recv, dp, zi):
        slot = (dp - 1) * nw + zi
        return pltpu.make_async_remote_copy(
            src_ref=src, dst_ref=dst, send_sem=send.at[slot], recv_sem=recv.at[slot],
            device_id={"planes": lax.rem(p + dp, np_)}, device_id_type=MESH)

    def lag_copy(k):
        return to_wide(lag_ref, lag_all.at[z], lag_s, lag_r, k)

    def x1_copy(dp, zi):
        return to_plane(part.at[lax.rem(p + dp, np_) * nw + zi], xrecv.at[(dp - 1) * nw + zi], x1_s, x1_r, dp, zi)

    def z1_copy(k):
        return to_wide(zsend.at[lax.rem(z + k, nw)], gath.at[z], z1_s, z1_r, k)

    def z2_copy(k):
        return to_wide(tbuf.at[lax.rem(z + k, nw)], tr_all.at[p * nw + z], z2_s, z2_r, k)

    def x2_copy(dp, zi):
        return to_plane(tr_all.at[p * nw + zi], tr_all.at[p * nw + zi], x2_s, x2_r, dp, zi)

    for k in range(1, nw):
        lag_copy(k).start()

    def smooth(n, carry):
        for u in range(step):
            q = n * step + u
            pi, f = q // frames, lax.rem(q, frames)
            spad[pi, f, edge : edge + rows] = jnp.dot(
                movie_ref[pi, f], col_fwd, preferred_element_type=F32).astype(BF)
        return carry

    lax.fori_loop(0, images // step, smooth, 0)
    here = lax.broadcasted_iota(jnp.int32, (rows, rows + 2 * edge), 0)
    there = lax.broadcasted_iota(jnp.int32, (rows, rows + 2 * edge), 1) - edge
    row_fwd = banded(row_ref, there - here + rim)
    halo_finish(in_copies, top_in, bot_in)
    for pi in range(planes_here):
        for held, at in ((top_in, 0), (bot_in, edge + rows)):
            spad[pi, :, at : at + edge] = jnp.dot(
                held[pi].reshape(frames * edge, width), col_fwd, preferred_element_type=F32
            ).astype(BF).reshape(frames, edge, width)
    mask_all = mask_ref[...].reshape(rows, width).astype(F32)

    def along(n, carry):
        for u in range(step):
            q = n * step + u
            pi, f = q // frames, lax.rem(q, frames)
            value = jnp.dot(row_fwd, spad[pi, f], preferred_element_type=F32) * mask_all
            cells[pi, pl.ds(f, rows, stride=frames), :] = value
        return carry

    lax.fori_loop(0, images // step, along, 0)

    def block_cells(b):
        span = pl.ds(b * hb * frames, hb * frames)
        return jnp.concatenate([cells[pi, span, :] for pi in range(planes_here)], axis=1).astype(BF)

    ids = lax.broadcasted_iota(jnp.int32, (tile, comps), 0)

    def project(b):
        base = b * hb
        f_blk = block_cells(b)
        pall[...] = lax.dot_general(
            f_blk, temp_ref[...], (((1,), (1,)), ((), ())), preferred_element_type=F32).astype(BF)
        sup = sup_ref[b]
        for i in range(hb):
            row = sup[i : i + 1, :]
            for q in range(0, shapes, tile):
                hot[base + i, q : q + tile, :] = jnp.where(ids == row - q, 1.0, 0.0).astype(BF)
            part[b, i] = jnp.dot(
                pall[i * frames : (i + 1) * frames, :], hot[base + i], preferred_element_type=F32).astype(BF)

    def others(n, carry):
        dp = n // nw + 1
        zi = lax.rem(z + 1 + n, nw)
        project(lax.rem(p + dp, np_) * nw + zi)
        x1_copy(dp, zi).start()
        return carry

    lax.fori_loop(0, (np_ - 1) * nw, others, 0)

    def mine(n, carry):
        zi = lax.rem(z + 1 + n, nw)
        b = p * nw + zi
        project(b)
        acc = part[b].astype(F32)
        for dp in range(1, np_):
            x1_copy(dp, zi).wait_recv()
            acc = acc + xrecv[(dp - 1) * nw + zi].astype(F32)
        zsend[zi] = acc.astype(BF)

        @pl.when(n < nw - 1)
        def _():
            z1_copy(n + 1).start()

        return carry

    lax.fori_loop(0, nw, mine, 0)
    gath[z] = zsend[z]

    def arrived(k, carry):
        lag_copy(k).wait()
        z1_copy(k).wait()
        return carry

    lax.fori_loop(1, nw, arrived, 0)

    me = p * nw + z
    for i in range(hb):
        table = lag_all[own_ref[me * hb + i]]
        columns = gath[:, i].reshape(total, comps)
        scores = jnp.dot(table, columns, preferred_element_type=F32)
        tbuf[:, i] = jnp.maximum(scores, 0.0).astype(BF).reshape(nw, frames, comps)

    def give(k, carry):
        z2_copy(k).start()
        return carry

    lax.fori_loop(1, nw, give, 0)
    tr_all[me] = tbuf[z]

    def model(b):
        base = b * hb
        for i in range(hb):
            fold[i * frames : (i + 1) * frames, :] = lax.dot_general(
                tr_all[b, i], hot[base + i], (((1,), (1,)), ((), ())), preferred_element_type=F32).astype(BF)
        tr_rows[pl.ds(base * frames, hb * frames), :] = tr_all[b].reshape(hb * frames, comps).astype(F32)
        out = jnp.dot(fold[...], temp_ref[...], preferred_element_type=F32)
        mask = mask_ref[b].astype(F32)
        mask = jnp.broadcast_to(mask[:, None, :], (hb, frames, width)).reshape(hb * frames, width)
        mask = jnp.concatenate([mask] * planes_here, axis=1)
        left = (block_cells(b).astype(F32) - mask * out).astype(BF).astype(F32)
        for pi in range(planes_here):
            cells[pi, pl.ds(base * frames, hb * frames), :] = left[:, pi * width : (pi + 1) * width]

    def same_plane(k, carry):
        zi = lax.rem(z + nw - k, nw)

        @pl.when(k > 0)
        def _():
            z2_copy(lax.max(k, 1)).wait_recv()

        for dp in range(1, np_):
            x2_copy(dp, zi).start()
        model(p * nw + zi)
        return carry

    lax.fori_loop(0, nw, same_plane, 0)

    def other_planes(n, carry):
        dp = n // nw + 1
        zi = lax.rem(z + nw - lax.rem(n, nw), nw)
        x2_copy(dp, zi).wait_recv()
        model(lax.rem(p + np_ - dp, np_) * nw + zi)
        return carry

    lax.fori_loop(0, (np_ - 1) * nw, other_planes, 0)

    def edges(n, carry):
        for u in range(step):
            q = n * step + u
            pi, f = q // frames, lax.rem(q, frames)
            for at in (0, rows - edge):
                spad[pi, f, edge + at : 2 * edge + at] = cells[
                    pi, pl.ds(f + at * frames, edge, stride=frames), :].astype(BF)
        return carry

    lax.fori_loop(0, images // step, edges, 0)
    out_copies = halo(spad, edge, rows, top_res, bot_res, 2)
    halo_start(out_copies)

    def inside(n, carry):
        for u in range(step):
            q = n * step + u
            pi, f = q // frames, lax.rem(q, frames)
            spad[pi, f, 2 * edge : rows] = cells[
                pi, pl.ds(f + edge * frames, rows - 2 * edge, stride=frames), :].astype(BF)
        return carry

    lax.fori_loop(0, images // step, inside, 0)

    share = comps // np_
    pick = (
        lax.broadcasted_iota(jnp.int32, (share, comps), 0) + p * share
        == lax.broadcasted_iota(jnp.int32, (share, comps), 1)
    )
    pick = jnp.where(pick, 1.0, 0.0).astype(BF)
    for t in range(frames):
        one = tr_rows[pl.ds(t, rows, stride=frames), :].astype(BF)
        tr_out[pl.ds(t, share, stride=frames), :] = lax.dot_general(
            pick, one, (((1,), (1,)), ((), ())), preferred_element_type=F32)
    tr_ref[...] = tr_out[...].astype(BF).reshape(tr_ref.shape)

    halo_finish(out_copies, top_res, bot_res)
    spad[:, :, 0:edge] = top_res[...]
    spad[:, :, edge + rows :] = bot_res[...]


    def drained_planes(n, carry):
        x1_copy(n // nw + 1, lax.rem(n, nw)).wait_send()
        x2_copy(n // nw + 1, lax.rem(n, nw)).wait_send()
        return carry

    lax.fori_loop(0, (np_ - 1) * nw, drained_planes, 0)

    def drained_wide(k, carry):
        z2_copy(k).wait_send()
        return carry

    lax.fori_loop(1, nw, drained_wide, 0)


def adjoint_kernel(rim, edge, pad_ref, tr_ref, row_ref, col_ref, back_ref, out_ref, row_adj, col_adj):
    rows, width = back_ref.shape[1:]

    @pl.when(pl.program_id(0) == 0)
    def _():
        here = lax.broadcasted_iota(jnp.int32, row_adj.shape, 0)
        there = lax.broadcasted_iota(jnp.int32, row_adj.shape, 1) - edge
        row_adj[...] = banded(row_ref, here - there + rim)
        inner = lax.broadcasted_iota(jnp.int32, (width, width), 0)
        outer = lax.broadcasted_iota(jnp.int32, (width, width), 1)
        col_adj[...] = banded(col_ref, outer - inner + rim)

    for q in range(back_ref.shape[0]):
        value = jnp.dot(row_adj[...], pad_ref[q], preferred_element_type=F32).astype(BF)
        back_ref[q] = jnp.dot(value, col_adj[...], preferred_element_type=F32).astype(BF)
    out_ref[...] = tr_ref[...]


def on_device(
    movie_frames, pixel_mask, tile_owner, support, templates, row_taps, col_taps, lag_gains, dilations
):
    np_ = lax.axis_size("planes")
    nw = lax.axis_size("wide")
    blocks = np_ * nw
    planes_here, frames, rows, width = movie_frames.shape
    hb = rows // blocks
    comps = support.shape[1]
    count = templates.shape[0]
    total = nw * frames
    rim = (row_taps.shape[0] - 1) // 2
    edge = -(-rim // 16) * 16
    vm = pl.BlockSpec(memory_space=pltpu.VMEM)
    sm = pl.BlockSpec(memory_space=pltpu.SMEM)
    dma = pltpu.SemaphoreType.DMA
    piece = (hb, frames, comps)
    across = (np_ - 1) * nw
    halo = pltpu.VMEM((planes_here, frames, edge, width), BF)
    padded = (planes_here * frames, rows + 2 * edge, width)
    held, traces = pl.pallas_call(
        kernel,
        out_shape=(
            jax.ShapeDtypeStruct((planes_here, frames) + padded[1:], BF),
            jax.ShapeDtypeStruct((comps // np_, frames, rows), BF),
        ),
        in_specs=[vm, vm, sm, vm, sm, sm, vm, sm, sm],
        out_specs=(vm, vm),
        scratch_shapes=[
            pltpu.VMEM((count, planes_here * width), BF),
            pltpu.VMEM((rows, count, comps), BF),
            pltpu.VMEM((hb * frames, count), BF),
            pltpu.VMEM((blocks,) + piece, BF),
            pltpu.VMEM((across,) + piece, BF),
            pltpu.VMEM((nw,) + piece, BF),
            pltpu.VMEM((nw,) + piece, BF),
            pltpu.VMEM((total, total), BF),
            pltpu.VMEM((nw, total, total), BF),
            pltpu.VMEM((nw,) + piece, BF),
            pltpu.VMEM((blocks,) + piece, BF),
            pltpu.VMEM((hb * frames, count), BF),
            halo, halo, halo, halo,
            pltpu.VMEM((planes_here, rows * frames, width), F32),
            pltpu.VMEM((rows * frames, comps), F32),
            pltpu.VMEM((comps // np_ * frames, rows), F32),
            dma((nw - 1,)), dma((nw - 1,)),
            dma((across,)), dma((across,)),
            dma((nw - 1,)), dma((nw - 1,)),
            dma((nw - 1,)), dma((nw - 1,)),
            dma((across,)), dma((across,)),
            dma((4,)), dma((4,)),
        ],
        compiler_params=pltpu.CompilerParams(
            collective_id=0, has_side_effects=True, vmem_limit_bytes=2 * (rows * count * comps + nw * total * total) + 24 * 1024 * 1024
        ),
    )(
        movie_frames,
        support.reshape(blocks, hb, comps),
        tile_owner[:, 0],
        templates,
        jnp.transpose(lag_gains, (1, 0, 2)),
        dilations,
        pixel_mask.reshape(blocks, hb, width),
        row_taps,
        col_taps,
    )
    steps = frames // 2
    few = padded[0] // steps
    share = traces.shape[0] // steps if traces.shape[0] % steps == 0 else 0
    part_spec = pl.BlockSpec((share,) + traces.shape[1:], lambda i: (i, 0, 0))
    back, traces = pl.pallas_call(
        functools.partial(adjoint_kernel, rim, edge),
        grid=(steps,),
        out_shape=(
            jax.ShapeDtypeStruct((padded[0], rows, width), BF),
            jax.ShapeDtypeStruct(traces.shape, BF),
        ),
        in_specs=[
            pl.BlockSpec((few,) + padded[1:], lambda i: (i, 0, 0)),
            part_spec,
            sm,
            sm,
        ],
        out_specs=(pl.BlockSpec((few, rows, width), lambda i: (i, 0, 0)), part_spec),
        scratch_shapes=[pltpu.VMEM((rows, rows + 2 * edge), BF), pltpu.VMEM((width, width), BF)],
        compiler_params=pltpu.CompilerParams(vmem_limit_bytes=16 * 1024 * 1024),
    )(held.reshape(padded), traces, row_taps, col_taps)
    return (traces, back.reshape(movie_frames.shape))


def solution(mesh):
    return jax.shard_map(
        on_device,
        mesh=mesh,
        in_specs=(
            P("planes", ("groups", "wide"), "rep", None),
            P("rep", None),
            P("rep", None),
            P("rep", None),
            P(None, "planes", None),
            P(),
            P(),
            P("wide", None, None),
            P("wide", None),
        ),
        out_specs=(
            P("planes", ("groups", "wide"), "rep"),
            P("planes", ("groups", "wide"), "rep", None),
        ),
        check_vma=False,
    )
```

```python
import functools

import jax
import jax.numpy as jnp
from jax import lax
from jax.experimental import pallas as pl
from jax.experimental.pallas import tpu as pltpu
from jax.sharding import PartitionSpec as P

MESH = pl.DeviceIdType.MESH
BF = jnp.bfloat16
F32 = jnp.float32


def banded(taps_ref, where_tap):
    out = jnp.zeros(where_tap.shape, F32)
    for k in range(taps_ref.shape[0]):
        out = jnp.where(where_tap == k, taps_ref[k], out)
    return out.astype(BF)


def lag_table(gain_ref, dil_ref, total):
    bands, _, taps = gain_ref.shape
    lag = lax.broadcasted_iota(jnp.int32, (1, 2 * total), 1) - (total - 1)
    row = jnp.zeros((1, 2 * total), F32)
    for b in range(bands):
        for k in range(taps):
            row = row + jnp.where(lag == dil_ref[0, b] * (k - (taps - 1) // 2), gain_ref[b, 0, k], 0.0)
    spread = jnp.broadcast_to(row, (total, 2 * total))
    return pltpu.roll(spread, total + 1, 1, stride=1, stride_axis=0)[:, :total].astype(BF)


def kernel(
    movie_ref, sup_ref, own_ref, table_ref, gain_ref, dil_ref, mask_ref, row_ref, col_ref,
    spad, tr_ref,
    temp_ref, hot, pall, part, xrecv, zsend, gath, lag_ref, lag_all, tbuf, tr_all, fold,
    top_in, bot_in, top_res, bot_res, cells, tr_rows, tr_out,
    lag_s, lag_r, x1_s, x1_r, z1_s, z1_r, z2_s, z2_r, x2_s, x2_r, h_s, h_r,
):
    np_ = lax.axis_size("planes")
    nw = lax.axis_size("wide")
    nr = lax.axis_size("rep")
    p = lax.axis_index("planes")
    z = lax.axis_index("wide")
    r = lax.axis_index("rep")
    blocks, hb, frames, comps = part.shape
    planes_here, _, rows, width = movie_ref.shape
    rim = (row_ref.shape[0] - 1) // 2
    edge = (spad.shape[2] - rows) // 2
    images = planes_here * frames
    shapes = temp_ref.shape[0]
    tile = min(256, shapes)
    total = nw * frames
    step = 4
    many = 8

    barrier = pltpu.get_barrier_semaphore()

    @pl.when(r > 0)
    def _():
        pl.semaphore_signal(barrier, inc=1, device_id={"rep": r - 1}, device_id_type=MESH)

    @pl.when(r < nr - 1)
    def _():
        pl.semaphore_signal(barrier, inc=1, device_id={"rep": r + 1}, device_id_type=MESH)

    for k in range(1, nw):
        pl.semaphore_signal(barrier, inc=1, device_id={"wide": lax.rem(z + k, nw)}, device_id_type=MESH)
    for k in range(1, np_):
        pl.semaphore_signal(barrier, inc=1, device_id={"planes": lax.rem(p + k, np_)}, device_id_type=MESH)

    lag_ref[...] = lag_table(gain_ref, dil_ref, total)
    lag_all[z] = lag_ref[...]
    for pi in range(planes_here):
        temp_ref[:, pi * width : (pi + 1) * width] = table_ref[:, pi, :]
    inner = lax.broadcasted_iota(jnp.int32, (width, width), 0)
    outer = lax.broadcasted_iota(jnp.int32, (width, width), 1)
    col_fwd = banded(col_ref, inner - outer + rim)

    pl.semaphore_wait(barrier, nw - 1 + np_ - 1 + lax.min(r, 1) + lax.min(nr - 1 - r, 1))

    def halo(source, lo, hi, top, bot, base):
        down = pltpu.make_async_remote_copy(
            src_ref=source.at[:, :, hi : hi + edge], dst_ref=top,
            send_sem=h_s.at[base], recv_sem=h_r.at[base],
            device_id={"rep": lax.min(r + 1, nr - 1)}, device_id_type=MESH)
        up = pltpu.make_async_remote_copy(
            src_ref=source.at[:, :, lo : lo + edge], dst_ref=bot,
            send_sem=h_s.at[base + 1], recv_sem=h_r.at[base + 1],
            device_id={"rep": lax.max(r - 1, 0)}, device_id_type=MESH)
        return down, up

    def halo_start(copies):
        @pl.when(r < nr - 1)
        def _():
            copies[0].start()

        @pl.when(r > 0)
        def _():
            copies[1].start()

    def halo_finish(copies, top, bot):
        @pl.when(r > 0)
        def _():
            copies[0].wait_recv()
            copies[1].wait_send()

        @pl.when(r == 0)
        def _():
            top[...] = jnp.zeros_like(top)

        @pl.when(r < nr - 1)
        def _():
            copies[1].wait_recv()
            copies[0].wait_send()

        @pl.when(r == nr - 1)
        def _():
            bot[...] = jnp.zeros_like(bot)

    in_copies = halo(movie_ref, 0, rows - edge, top_in, bot_in, 0)
    halo_start(in_copies)

    def to_wide(src, dst, send, recv, k):
        return pltpu.make_async_remote_copy(
            src_ref=src, dst_ref=dst, send_sem=send.at[k - 1], recv_sem=recv.at[k - 1],
            device_id={"wide": lax.rem(z + k, nw)}, device_id_type=MESH)

    def to_plane(src, dst, send, recv, dp, zi):
        slot = (dp - 1) * nw + zi
        return pltpu.make_async_remote_copy(
            src_ref=src, dst_ref=dst, send_sem=send.at[slot], recv_sem=recv.at[slot],
            device_id={"planes": lax.rem(p + dp, np_)}, device_id_type=MESH)

    def lag_copy(k):
        return to_wide(lag_ref, lag_all.at[z], lag_s, lag_r, k)

    def x1_copy(dp, zi):
        return to_plane(part.at[lax.rem(p + dp, np_) * nw + zi], xrecv.at[(dp - 1) * nw + zi], x1_s, x1_r, dp, zi)

    def z1_copy(k):
        return to_wide(zsend.at[lax.rem(z + k, nw)], gath.at[z], z1_s, z1_r, k)

    def z2_copy(k):
        return to_wide(tbuf.at[lax.rem(z + k, nw)], tr_all.at[p * nw + z], z2_s, z2_r, k)

    def x2_copy(dp, zi):
        return to_plane(tr_all.at[p * nw + zi], tr_all.at[p * nw + zi], x2_s, x2_r, dp, zi)

    for k in range(1, nw):
        lag_copy(k).start()

    def smooth(n, carry):
        pi, f = n * many // frames, lax.rem(n * many, frames)
        spad[pi, pl.ds(f, many), edge : edge + rows] = jnp.dot(
            movie_ref[pi, pl.ds(f, many)].reshape(many * rows, width), col_fwd, preferred_element_type=F32
        ).astype(BF).reshape(many, rows, width)
        return carry

    lax.fori_loop(0, images // many, smooth, 0)
    here = lax.broadcasted_iota(jnp.int32, (rows, rows + 2 * edge), 0)
    there = lax.broadcasted_iota(jnp.int32, (rows, rows + 2 * edge), 1) - edge
    row_fwd = banded(row_ref, there - here + rim)
    halo_finish(in_copies, top_in, bot_in)
    for pi in range(planes_here):
        for held, at in ((top_in, 0), (bot_in, edge + rows)):
            spad[pi, :, at : at + edge] = jnp.dot(
                held[pi].reshape(frames * edge, width), col_fwd, preferred_element_type=F32
            ).astype(BF).reshape(frames, edge, width)
    mask_all = mask_ref[...].reshape(rows, width).astype(F32)

    def along(n, carry):
        for u in range(0, many, 2):
            q = n * many + u
            pi, f = q // frames, lax.rem(q, frames)
            pair = jnp.concatenate([spad[pi, f], spad[pi, f + 1]], axis=1)
            value = jnp.dot(row_fwd, pair, preferred_element_type=F32)
            for v in range(2):
                cells[pi, pl.ds(f + v, rows, stride=frames), :] = (
                    value[:, v * width : (v + 1) * width] * mask_all)
        return carry

    lax.fori_loop(0, images // many, along, 0)

    def block_cells(b):
        span = pl.ds(b * hb * frames, hb * frames)
        return jnp.concatenate([cells[pi, span, :] for pi in range(planes_here)], axis=1).astype(BF)

    ids = lax.broadcasted_iota(jnp.int32, (tile, comps), 0)

    def project(b):
        base = b * hb
        f_blk = block_cells(b)
        pall[...] = lax.dot_general(
            f_blk, temp_ref[...], (((1,), (1,)), ((), ())), preferred_element_type=F32).astype(BF)
        sup = sup_ref[b]
        for i in range(hb):
            row = sup[i : i + 1, :]
            for q in range(0, shapes, tile):
                hot[base + i, q : q + tile, :] = jnp.where(ids == row - q, 1.0, 0.0).astype(BF)
            part[b, i] = jnp.dot(
                pall[i * frames : (i + 1) * frames, :], hot[base + i], preferred_element_type=F32).astype(BF)

    def others(n, carry):
        dp = n // nw + 1
        zi = lax.rem(z + 1 + n, nw)
        project(lax.rem(p + dp, np_) * nw + zi)
        x1_copy(dp, zi).start()
        return carry

    lax.fori_loop(0, (np_ - 1) * nw, others, 0)

    def mine(n, carry):
        zi = lax.rem(z + 1 + n, nw)
        b = p * nw + zi
        project(b)
        acc = part[b].astype(F32)
        for dp in range(1, np_):
            x1_copy(dp, zi).wait_recv()
            acc = acc + xrecv[(dp - 1) * nw + zi].astype(F32)
        zsend[zi] = acc.astype(BF)

        @pl.when(n < nw - 1)
        def _():
            z1_copy(n + 1).start()

        return carry

    lax.fori_loop(0, nw, mine, 0)
    gath[z] = zsend[z]

    def arrived(k, carry):
        lag_copy(k).wait()
        z1_copy(k).wait()
        return carry

    lax.fori_loop(1, nw, arrived, 0)

    me = p * nw + z
    for i in range(hb):
        table = lag_all[own_ref[me * hb + i]]
        columns = gath[:, i].reshape(total, comps)
        scores = jnp.dot(table, columns, preferred_element_type=F32)
        tbuf[:, i] = jnp.maximum(scores, 0.0).astype(BF).reshape(nw, frames, comps)

    def give(k, carry):
        z2_copy(k).start()
        return carry

    lax.fori_loop(1, nw, give, 0)
    tr_all[me] = tbuf[z]

    def model(b):
        base = b * hb
        for i in range(hb):
            fold[i * frames : (i + 1) * frames, :] = lax.dot_general(
                tr_all[b, i], hot[base + i], (((1,), (1,)), ((), ())), preferred_element_type=F32).astype(BF)
        tr_rows[pl.ds(base * frames, hb * frames), :] = tr_all[b].reshape(hb * frames, comps).astype(F32)
        out = jnp.dot(fold[...], temp_ref[...], preferred_element_type=F32)
        mask = mask_ref[b].astype(F32)
        mask = jnp.broadcast_to(mask[:, None, :], (hb, frames, width)).reshape(hb * frames, width)
        mask = jnp.concatenate([mask] * planes_here, axis=1)
        left = (block_cells(b).astype(F32) - mask * out).astype(BF).astype(F32)
        for pi in range(planes_here):
            cells[pi, pl.ds(base * frames, hb * frames), :] = left[:, pi * width : (pi + 1) * width]

    def same_plane(k, carry):
        zi = lax.rem(z + nw - k, nw)

        @pl.when(k > 0)
        def _():
            z2_copy(lax.max(k, 1)).wait_recv()

        for dp in range(1, np_):
            x2_copy(dp, zi).start()
        model(p * nw + zi)
        return carry

    lax.fori_loop(0, nw, same_plane, 0)

    def other_planes(n, carry):
        dp = n // nw + 1
        zi = lax.rem(z + nw - lax.rem(n, nw), nw)
        x2_copy(dp, zi).wait_recv()
        model(lax.rem(p + np_ - dp, np_) * nw + zi)
        return carry

    lax.fori_loop(0, (np_ - 1) * nw, other_planes, 0)

    def edges(n, carry):
        for u in range(step):
            q = n * step + u
            pi, f = q // frames, lax.rem(q, frames)
            for at in (0, rows - edge):
                spad[pi, f, edge + at : 2 * edge + at] = cells[
                    pi, pl.ds(f + at * frames, edge, stride=frames), :].astype(BF)
        return carry

    lax.fori_loop(0, images // step, edges, 0)
    out_copies = halo(spad, edge, rows, top_res, bot_res, 2)
    halo_start(out_copies)

    def inside(n, carry):
        for u in range(step):
            q = n * step + u
            pi, f = q // frames, lax.rem(q, frames)
            spad[pi, f, 2 * edge : rows] = cells[
                pi, pl.ds(f + edge * frames, rows - 2 * edge, stride=frames), :].astype(BF)
        return carry

    lax.fori_loop(0, images // step, inside, 0)

    share = comps // np_
    pick = (
        lax.broadcasted_iota(jnp.int32, (share, comps), 0) + p * share
        == lax.broadcasted_iota(jnp.int32, (share, comps), 1)
    )
    pick = jnp.where(pick, 1.0, 0.0).astype(BF)
    for t in range(frames):
        one = tr_rows[pl.ds(t, rows, stride=frames), :].astype(BF)
        tr_out[pl.ds(t, share, stride=frames), :] = lax.dot_general(
            pick, one, (((1,), (1,)), ((), ())), preferred_element_type=F32)
    tr_ref[...] = tr_out[...].astype(BF).reshape(tr_ref.shape)

    halo_finish(out_copies, top_res, bot_res)
    spad[:, :, 0:edge] = top_res[...]
    spad[:, :, edge + rows :] = bot_res[...]


    def drained_planes(n, carry):
        x1_copy(n // nw + 1, lax.rem(n, nw)).wait_send()
        x2_copy(n // nw + 1, lax.rem(n, nw)).wait_send()
        return carry

    lax.fori_loop(0, (np_ - 1) * nw, drained_planes, 0)

    def drained_wide(k, carry):
        z2_copy(k).wait_send()
        return carry

    lax.fori_loop(1, nw, drained_wide, 0)


def adjoint_kernel(rim, edge, pad_ref, tr_ref, row_ref, col_ref, back_ref, out_ref, row_adj, col_adj):
    rows, width = back_ref.shape[1:]

    @pl.when(pl.program_id(0) == 0)
    def _():
        here = lax.broadcasted_iota(jnp.int32, row_adj.shape, 0)
        there = lax.broadcasted_iota(jnp.int32, row_adj.shape, 1) - edge
        row_adj[...] = banded(row_ref, here - there + rim)
        inner = lax.broadcasted_iota(jnp.int32, (width, width), 0)
        outer = lax.broadcasted_iota(jnp.int32, (width, width), 1)
        col_adj[...] = banded(col_ref, outer - inner + rim)

    count = back_ref.shape[0]
    parts = []
    for q in range(0, count, 2):
        pair = jnp.concatenate([pad_ref[q], pad_ref[q + 1]], axis=1)
        value = jnp.dot(row_adj[...], pair, preferred_element_type=F32).astype(BF)
        parts += [value[:, :width], value[:, width:]]
    back_ref[...] = jnp.dot(
        jnp.concatenate(parts, axis=0), col_adj[...], preferred_element_type=F32
    ).astype(BF).reshape(count, rows, width)
    out_ref[...] = tr_ref[...]


def on_device(
    movie_frames, pixel_mask, tile_owner, support, templates, row_taps, col_taps, lag_gains, dilations
):
    np_ = lax.axis_size("planes")
    nw = lax.axis_size("wide")
    blocks = np_ * nw
    planes_here, frames, rows, width = movie_frames.shape
    hb = rows // blocks
    comps = support.shape[1]
    count = templates.shape[0]
    total = nw * frames
    rim = (row_taps.shape[0] - 1) // 2
    edge = -(-rim // 16) * 16
    vm = pl.BlockSpec(memory_space=pltpu.VMEM)
    sm = pl.BlockSpec(memory_space=pltpu.SMEM)
    dma = pltpu.SemaphoreType.DMA
    piece = (hb, frames, comps)
    across = (np_ - 1) * nw
    halo = pltpu.VMEM((planes_here, frames, edge, width), BF)
    padded = (planes_here * frames, rows + 2 * edge, width)
    held, traces = pl.pallas_call(
        kernel,
        out_shape=(
            jax.ShapeDtypeStruct((planes_here, frames) + padded[1:], BF),
            jax.ShapeDtypeStruct((comps // np_, frames, rows), BF),
        ),
        in_specs=[vm, vm, sm, vm, sm, sm, vm, sm, sm],
        out_specs=(vm, vm),
        scratch_shapes=[
            pltpu.VMEM((count, planes_here * width), BF),
            pltpu.VMEM((rows, count, comps), BF),
            pltpu.VMEM((hb * frames, count), BF),
            pltpu.VMEM((blocks,) + piece, BF),
            pltpu.VMEM((across,) + piece, BF),
            pltpu.VMEM((nw,) + piece, BF),
            pltpu.VMEM((nw,) + piece, BF),
            pltpu.VMEM((total, total), BF),
            pltpu.VMEM((nw, total, total), BF),
            pltpu.VMEM((nw,) + piece, BF),
            pltpu.VMEM((blocks,) + piece, BF),
            pltpu.VMEM((hb * frames, count), BF),
            halo, halo, halo, halo,
            pltpu.VMEM((planes_here, rows * frames, width), F32),
            pltpu.VMEM((rows * frames, comps), F32),
            pltpu.VMEM((comps // np_ * frames, rows), F32),
            dma((nw - 1,)), dma((nw - 1,)),
            dma((across,)), dma((across,)),
            dma((nw - 1,)), dma((nw - 1,)),
            dma((nw - 1,)), dma((nw - 1,)),
            dma((across,)), dma((across,)),
            dma((4,)), dma((4,)),
        ],
        compiler_params=pltpu.CompilerParams(
            collective_id=0, has_side_effects=True, vmem_limit_bytes=63 * 1024 * 1024
        ),
    )(
        movie_frames,
        support.reshape(blocks, hb, comps),
        tile_owner[:, 0],
        templates,
        jnp.transpose(lag_gains, (1, 0, 2)),
        dilations,
        pixel_mask.reshape(blocks, hb, width),
        row_taps,
        col_taps,
    )
    steps = frames // 4
    few = padded[0] // steps
    share = traces.shape[0] // steps if traces.shape[0] % steps == 0 else 0
    part_spec = pl.BlockSpec((share,) + traces.shape[1:], lambda i: (i, 0, 0))
    back, traces = pl.pallas_call(
        functools.partial(adjoint_kernel, rim, edge),
        grid=(steps,),
        out_shape=(
            jax.ShapeDtypeStruct((padded[0], rows, width), BF),
            jax.ShapeDtypeStruct(traces.shape, BF),
        ),
        in_specs=[
            pl.BlockSpec((few,) + padded[1:], lambda i: (i, 0, 0)),
            part_spec,
            sm,
            sm,
        ],
        out_specs=(pl.BlockSpec((few, rows, width), lambda i: (i, 0, 0)), part_spec),
        scratch_shapes=[pltpu.VMEM((rows, rows + 2 * edge), BF), pltpu.VMEM((width, width), BF)],
        compiler_params=pltpu.CompilerParams(vmem_limit_bytes=63 * 1024 * 1024),
    )(held.reshape(padded), traces, row_taps, col_taps)
    return (traces, back.reshape(movie_frames.shape))


def solution(mesh):
    return jax.shard_map(
        on_device,
        mesh=mesh,
        in_specs=(
            P("planes", ("groups", "wide"), "rep", None),
            P("rep", None),
            P("rep", None),
            P("rep", None),
            P(None, "planes", None),
            P(),
            P(),
            P("wide", None, None),
            P("wide", None),
        ),
        out_specs=(
            P("planes", ("groups", "wide"), "rep"),
            P("planes", ("groups", "wide"), "rep", None),
        ),
        check_vma=False,
    )
```

```python
import functools

import jax
import jax.numpy as jnp
from jax import lax
from jax.experimental import pallas as pl
from jax.experimental.pallas import tpu as pltpu
from jax.sharding import PartitionSpec as P

MESH = pl.DeviceIdType.MESH
BF = jnp.bfloat16
F32 = jnp.float32


def banded(taps_ref, where_tap):
    out = jnp.zeros(where_tap.shape, F32)
    for k in range(taps_ref.shape[0]):
        out = jnp.where(where_tap == k, taps_ref[k], out)
    return out.astype(BF)


def lag_table(gain_ref, dil_ref, total):
    bands, _, taps = gain_ref.shape
    lag = lax.broadcasted_iota(jnp.int32, (1, 2 * total), 1) - (total - 1)
    row = jnp.zeros((1, 2 * total), F32)
    for b in range(bands):
        for k in range(taps):
            row = row + jnp.where(lag == dil_ref[0, b] * (k - (taps - 1) // 2), gain_ref[b, 0, k], 0.0)
    spread = jnp.broadcast_to(row, (total, 2 * total))
    return pltpu.roll(spread, total + 1, 1, stride=1, stride_axis=0)[:, :total].astype(BF)


def kernel(
    movie_ref, sup_ref, own_ref, table_ref, gain_ref, dil_ref, mask_ref, row_ref, col_ref,
    spad, tr_ref,
    temp_ref, hot, pall, part, xrecv, zsend, gath, lag_ref, lag_all, tbuf, tr_all, fold,
    top_in, bot_in, top_res, bot_res, cells, tr_rows, tr_out,
    lag_s, lag_r, x1_s, x1_r, z1_s, z1_r, z2_s, z2_r, x2_s, x2_r, h_s, h_r,
):
    np_ = lax.axis_size("planes")
    nw = lax.axis_size("wide")
    nr = lax.axis_size("rep")
    p = lax.axis_index("planes")
    z = lax.axis_index("wide")
    r = lax.axis_index("rep")
    blocks, hb, frames, comps = part.shape
    planes_here, _, rows, width = movie_ref.shape
    rim = (row_ref.shape[0] - 1) // 2
    edge = (spad.shape[2] - rows) // 2
    images = planes_here * frames
    shapes = temp_ref.shape[0]
    tile = min(256, shapes)
    total = nw * frames
    step = 4
    many = 8

    barrier = pltpu.get_barrier_semaphore()

    @pl.when(r > 0)
    def _():
        pl.semaphore_signal(barrier, inc=1, device_id={"rep": r - 1}, device_id_type=MESH)

    @pl.when(r < nr - 1)
    def _():
        pl.semaphore_signal(barrier, inc=1, device_id={"rep": r + 1}, device_id_type=MESH)

    for k in range(1, nw):
        pl.semaphore_signal(barrier, inc=1, device_id={"wide": lax.rem(z + k, nw)}, device_id_type=MESH)
    for k in range(1, np_):
        pl.semaphore_signal(barrier, inc=1, device_id={"planes": lax.rem(p + k, np_)}, device_id_type=MESH)

    lag_ref[...] = lag_table(gain_ref, dil_ref, total)
    lag_all[z] = lag_ref[...]
    inner = lax.broadcasted_iota(jnp.int32, (width, width), 0)
    outer = lax.broadcasted_iota(jnp.int32, (width, width), 1)
    col_fwd = banded(col_ref, inner - outer + rim)

    pl.semaphore_wait(barrier, nw - 1 + np_ - 1 + lax.min(r, 1) + lax.min(nr - 1 - r, 1))

    def halo(source, lo, hi, top, bot, base):
        down = pltpu.make_async_remote_copy(
            src_ref=source.at[:, :, hi : hi + edge], dst_ref=top,
            send_sem=h_s.at[base], recv_sem=h_r.at[base],
            device_id={"rep": lax.min(r + 1, nr - 1)}, device_id_type=MESH)
        up = pltpu.make_async_remote_copy(
            src_ref=source.at[:, :, lo : lo + edge], dst_ref=bot,
            send_sem=h_s.at[base + 1], recv_sem=h_r.at[base + 1],
            device_id={"rep": lax.max(r - 1, 0)}, device_id_type=MESH)
        return down, up

    def halo_start(copies):
        @pl.when(r < nr - 1)
        def _():
            copies[0].start()

        @pl.when(r > 0)
        def _():
            copies[1].start()

    def halo_finish(copies, top, bot):
        @pl.when(r > 0)
        def _():
            copies[0].wait_recv()
            copies[1].wait_send()

        @pl.when(r == 0)
        def _():
            top[...] = jnp.zeros_like(top)

        @pl.when(r < nr - 1)
        def _():
            copies[1].wait_recv()
            copies[0].wait_send()

        @pl.when(r == nr - 1)
        def _():
            bot[...] = jnp.zeros_like(bot)

    in_copies = halo(movie_ref, 0, rows - edge, top_in, bot_in, 0)
    halo_start(in_copies)
    for pi in range(planes_here):
        temp_ref[:, pi * width : (pi + 1) * width] = table_ref[:, pi, :]

    def to_wide(src, dst, send, recv, k):
        return pltpu.make_async_remote_copy(
            src_ref=src, dst_ref=dst, send_sem=send.at[k - 1], recv_sem=recv.at[k - 1],
            device_id={"wide": lax.rem(z + k, nw)}, device_id_type=MESH)

    def to_plane(src, dst, send, recv, dp, zi):
        slot = (dp - 1) * nw + zi
        return pltpu.make_async_remote_copy(
            src_ref=src, dst_ref=dst, send_sem=send.at[slot], recv_sem=recv.at[slot],
            device_id={"planes": lax.rem(p + dp, np_)}, device_id_type=MESH)

    def lag_copy(k):
        return to_wide(lag_ref, lag_all.at[z], lag_s, lag_r, k)

    def x1_copy(dp, zi):
        return to_plane(part.at[lax.rem(p + dp, np_) * nw + zi], xrecv.at[(dp - 1) * nw + zi], x1_s, x1_r, dp, zi)

    def z1_copy(k):
        return to_wide(zsend.at[lax.rem(z + k, nw)], gath.at[z], z1_s, z1_r, k)

    def z2_copy(k):
        return to_wide(tbuf.at[lax.rem(z + k, nw)], tr_all.at[p * nw + z], z2_s, z2_r, k)

    def x2_copy(dp, zi):
        return to_plane(tr_all.at[p * nw + zi], tr_all.at[p * nw + zi], x2_s, x2_r, dp, zi)

    for k in range(1, nw):
        lag_copy(k).start()

    def smooth(n, carry):
        pi, f = n * many // frames, lax.rem(n * many, frames)
        spad[pi, pl.ds(f, many), edge : edge + rows] = jnp.dot(
            movie_ref[pi, pl.ds(f, many)].reshape(many * rows, width), col_fwd, preferred_element_type=F32
        ).astype(BF).reshape(many, rows, width)
        return carry

    lax.fori_loop(0, images // many, smooth, 0)
    here = lax.broadcasted_iota(jnp.int32, (rows, rows + 2 * edge), 0)
    there = lax.broadcasted_iota(jnp.int32, (rows, rows + 2 * edge), 1) - edge
    row_fwd = banded(row_ref, there - here + rim)
    halo_finish(in_copies, top_in, bot_in)
    for pi in range(planes_here):
        for held, at in ((top_in, 0), (bot_in, edge + rows)):
            spad[pi, :, at : at + edge] = jnp.dot(
                held[pi].reshape(frames * edge, width), col_fwd, preferred_element_type=F32
            ).astype(BF).reshape(frames, edge, width)
    mask_all = mask_ref[...].reshape(rows, width).astype(F32)

    def along(n, carry):
        for u in range(0, many, 2):
            q = n * many + u
            pi, f = q // frames, lax.rem(q, frames)
            pair = jnp.concatenate([spad[pi, f], spad[pi, f + 1]], axis=1)
            value = jnp.dot(row_fwd, pair, preferred_element_type=F32)
            for v in range(2):
                cells[pi, pl.ds(f + v, rows, stride=frames), :] = (
                    value[:, v * width : (v + 1) * width] * mask_all)
        return carry

    lax.fori_loop(0, images // many, along, 0)

    def block_cells(b):
        span = pl.ds(b * hb * frames, hb * frames)
        return jnp.concatenate([cells[pi, span, :] for pi in range(planes_here)], axis=1).astype(BF)

    ids = lax.broadcasted_iota(jnp.int32, (tile, comps), 0).astype(F32).astype(BF)
    one, none = jnp.ones((), BF), jnp.zeros((), BF)

    def project(b):
        base = b * hb
        f_blk = block_cells(b)
        pall[...] = lax.dot_general(
            f_blk, temp_ref[...], (((1,), (1,)), ((), ())), preferred_element_type=F32).astype(BF)
        sup = sup_ref[b]
        for i in range(hb):
            row = sup[i : i + 1, :]
            marks = jnp.concatenate(
                [
                    jnp.where(ids == (row - q).astype(F32).astype(BF), one, none)
                    for q in range(0, shapes, tile)
                ],
                axis=0,
            )
            hot[base + i] = marks
            part[b, i] = jnp.dot(
                pall[i * frames : (i + 1) * frames, :], marks, preferred_element_type=F32).astype(BF)

    def others(n, carry):
        dp = n // nw + 1
        zi = lax.rem(z + 1 + n, nw)
        project(lax.rem(p + dp, np_) * nw + zi)
        x1_copy(dp, zi).start()
        return carry

    lax.fori_loop(0, (np_ - 1) * nw, others, 0)

    def mine(n, carry):
        zi = lax.rem(z + 1 + n, nw)
        b = p * nw + zi
        project(b)
        acc = part[b].astype(F32)
        for dp in range(1, np_):
            x1_copy(dp, zi).wait_recv()
            acc = acc + xrecv[(dp - 1) * nw + zi].astype(F32)
        zsend[zi] = acc.astype(BF)

        @pl.when(n < nw - 1)
        def _():
            z1_copy(n + 1).start()

        return carry

    lax.fori_loop(0, nw, mine, 0)
    gath[z] = zsend[z]

    def arrived(k, carry):
        lag_copy(k).wait()
        z1_copy(k).wait()
        return carry

    lax.fori_loop(1, nw, arrived, 0)

    me = p * nw + z
    for i in range(hb):
        table = lag_all[own_ref[me * hb + i]]
        columns = gath[:, i].reshape(total, comps)
        scores = jnp.dot(table, columns, preferred_element_type=F32)
        tbuf[:, i] = jnp.maximum(scores, 0.0).astype(BF).reshape(nw, frames, comps)

    def give(k, carry):
        z2_copy(k).start()
        return carry

    lax.fori_loop(1, nw, give, 0)
    tr_all[me] = tbuf[z]

    def model(b):
        base = b * hb
        for i in range(hb):
            fold[i * frames : (i + 1) * frames, :] = lax.dot_general(
                tr_all[b, i], hot[base + i], (((1,), (1,)), ((), ())), preferred_element_type=F32).astype(BF)
        tr_rows[pl.ds(base * frames, hb * frames), :] = tr_all[b].reshape(hb * frames, comps).astype(F32)
        out = jnp.dot(fold[...], temp_ref[...], preferred_element_type=F32)
        mask = mask_ref[b].astype(F32)
        mask = jnp.broadcast_to(mask[:, None, :], (hb, frames, width)).reshape(hb * frames, width)
        mask = jnp.concatenate([mask] * planes_here, axis=1)
        left = (block_cells(b).astype(F32) - mask * out).astype(BF).astype(F32)
        for pi in range(planes_here):
            cells[pi, pl.ds(base * frames, hb * frames), :] = left[:, pi * width : (pi + 1) * width]

    def same_plane(k, carry):
        zi = lax.rem(z + nw - k, nw)

        @pl.when(k > 0)
        def _():
            z2_copy(lax.max(k, 1)).wait_recv()

        for dp in range(1, np_):
            x2_copy(dp, zi).start()
        model(p * nw + zi)
        return carry

    lax.fori_loop(0, nw, same_plane, 0)

    def other_planes(n, carry):
        dp = n // nw + 1
        zi = lax.rem(z + nw - lax.rem(n, nw), nw)
        x2_copy(dp, zi).wait_recv()
        model(lax.rem(p + np_ - dp, np_) * nw + zi)
        return carry

    lax.fori_loop(0, (np_ - 1) * nw, other_planes, 0)

    def edges(n, carry):
        for u in range(step):
            q = n * step + u
            pi, f = q // frames, lax.rem(q, frames)
            for at in (0, rows - edge):
                spad[pi, f, edge + at : 2 * edge + at] = cells[
                    pi, pl.ds(f + at * frames, edge, stride=frames), :].astype(BF)
        return carry

    lax.fori_loop(0, images // step, edges, 0)
    out_copies = halo(spad, edge, rows, top_res, bot_res, 2)
    halo_start(out_copies)

    def inside(n, carry):
        for u in range(step):
            q = n * step + u
            pi, f = q // frames, lax.rem(q, frames)
            spad[pi, f, 2 * edge : rows] = cells[
                pi, pl.ds(f + edge * frames, rows - 2 * edge, stride=frames), :].astype(BF)
        return carry

    lax.fori_loop(0, images // step, inside, 0)

    share = comps // np_
    pick = (
        lax.broadcasted_iota(jnp.int32, (share, comps), 0) + p * share
        == lax.broadcasted_iota(jnp.int32, (share, comps), 1)
    )
    pick = jnp.where(pick, 1.0, 0.0).astype(BF)
    for t in range(frames):
        one = tr_rows[pl.ds(t, rows, stride=frames), :].astype(BF)
        tr_out[pl.ds(t, share, stride=frames), :] = lax.dot_general(
            pick, one, (((1,), (1,)), ((), ())), preferred_element_type=F32)
    tr_ref[...] = tr_out[...].astype(BF).reshape(tr_ref.shape)

    halo_finish(out_copies, top_res, bot_res)
    spad[:, :, 0:edge] = top_res[...]
    spad[:, :, edge + rows :] = bot_res[...]


    def drained_planes(n, carry):
        x1_copy(n // nw + 1, lax.rem(n, nw)).wait_send()
        x2_copy(n // nw + 1, lax.rem(n, nw)).wait_send()
        return carry

    lax.fori_loop(0, (np_ - 1) * nw, drained_planes, 0)

    def drained_wide(k, carry):
        z2_copy(k).wait_send()
        return carry

    lax.fori_loop(1, nw, drained_wide, 0)


def adjoint_kernel(rim, edge, pad_ref, tr_ref, row_ref, col_ref, back_ref, out_ref, row_adj, col_adj):
    rows, width = back_ref.shape[1:]

    @pl.when(pl.program_id(0) == 0)
    def _():
        here = lax.broadcasted_iota(jnp.int32, row_adj.shape, 0)
        there = lax.broadcasted_iota(jnp.int32, row_adj.shape, 1) - edge
        row_adj[...] = banded(row_ref, here - there + rim)
        inner = lax.broadcasted_iota(jnp.int32, (width, width), 0)
        outer = lax.broadcasted_iota(jnp.int32, (width, width), 1)
        col_adj[...] = banded(col_ref, outer - inner + rim)

    count = back_ref.shape[0]
    parts = []
    for q in range(0, count, 2):
        pair = jnp.concatenate([pad_ref[q], pad_ref[q + 1]], axis=1)
        value = jnp.dot(row_adj[...], pair, preferred_element_type=F32).astype(BF)
        parts += [value[:, :width], value[:, width:]]
    back_ref[...] = jnp.dot(
        jnp.concatenate(parts, axis=0), col_adj[...], preferred_element_type=F32
    ).astype(BF).reshape(count, rows, width)
    out_ref[...] = tr_ref[...]


def on_device(
    movie_frames, pixel_mask, tile_owner, support, templates, row_taps, col_taps, lag_gains, dilations
):
    np_ = lax.axis_size("planes")
    nw = lax.axis_size("wide")
    blocks = np_ * nw
    planes_here, frames, rows, width = movie_frames.shape
    hb = rows // blocks
    comps = support.shape[1]
    count = templates.shape[0]
    total = nw * frames
    rim = (row_taps.shape[0] - 1) // 2
    edge = -(-rim // 16) * 16
    vm = pl.BlockSpec(memory_space=pltpu.VMEM)
    sm = pl.BlockSpec(memory_space=pltpu.SMEM)
    dma = pltpu.SemaphoreType.DMA
    piece = (hb, frames, comps)
    across = (np_ - 1) * nw
    halo = pltpu.VMEM((planes_here, frames, edge, width), BF)
    padded = (planes_here * frames, rows + 2 * edge, width)
    held, traces = pl.pallas_call(
        kernel,
        out_shape=(
            jax.ShapeDtypeStruct((planes_here, frames) + padded[1:], BF),
            jax.ShapeDtypeStruct((comps // np_, frames, rows), BF),
        ),
        in_specs=[vm, vm, sm, vm, sm, sm, vm, sm, sm],
        out_specs=(vm, vm),
        scratch_shapes=[
            pltpu.VMEM((count, planes_here * width), BF),
            pltpu.VMEM((rows, count, comps), BF),
            pltpu.VMEM((hb * frames, count), BF),
            pltpu.VMEM((blocks,) + piece, BF),
            pltpu.VMEM((across,) + piece, BF),
            pltpu.VMEM((nw,) + piece, BF),
            pltpu.VMEM((nw,) + piece, BF),
            pltpu.VMEM((total, total), BF),
            pltpu.VMEM((nw, total, total), BF),
            pltpu.VMEM((nw,) + piece, BF),
            pltpu.VMEM((blocks,) + piece, BF),
            pltpu.VMEM((hb * frames, count), BF),
            halo, halo, halo, halo,
            pltpu.VMEM((planes_here, rows * frames, width), F32),
            pltpu.VMEM((rows * frames, comps), F32),
            pltpu.VMEM((comps // np_ * frames, rows), F32),
            dma((nw - 1,)), dma((nw - 1,)),
            dma((across,)), dma((across,)),
            dma((nw - 1,)), dma((nw - 1,)),
            dma((nw - 1,)), dma((nw - 1,)),
            dma((across,)), dma((across,)),
            dma((4,)), dma((4,)),
        ],
        compiler_params=pltpu.CompilerParams(
            collective_id=0, has_side_effects=True, vmem_limit_bytes=63 * 1024 * 1024
        ),
    )(
        movie_frames,
        support.reshape(blocks, hb, comps),
        tile_owner[:, 0],
        templates,
        jnp.transpose(lag_gains, (1, 0, 2)),
        dilations,
        pixel_mask.reshape(blocks, hb, width),
        row_taps,
        col_taps,
    )
    steps = frames // 4
    few = padded[0] // steps
    share = traces.shape[0] // steps if traces.shape[0] % steps == 0 else 0
    part_spec = pl.BlockSpec((share,) + traces.shape[1:], lambda i: (i, 0, 0))
    back, traces = pl.pallas_call(
        functools.partial(adjoint_kernel, rim, edge),
        grid=(steps,),
        out_shape=(
            jax.ShapeDtypeStruct((padded[0], rows, width), BF),
            jax.ShapeDtypeStruct(traces.shape, BF),
        ),
        in_specs=[
            pl.BlockSpec((few,) + padded[1:], lambda i: (i, 0, 0)),
            part_spec,
            sm,
            sm,
        ],
        out_specs=(pl.BlockSpec((few, rows, width), lambda i: (i, 0, 0)), part_spec),
        scratch_shapes=[pltpu.VMEM((rows, rows + 2 * edge), BF), pltpu.VMEM((width, width), BF)],
        compiler_params=pltpu.CompilerParams(vmem_limit_bytes=63 * 1024 * 1024),
    )(held.reshape(padded), traces, row_taps, col_taps)
    return (traces, back.reshape(movie_frames.shape))


def solution(mesh):
    return jax.shard_map(
        on_device,
        mesh=mesh,
        in_specs=(
            P("planes", ("groups", "wide"), "rep", None),
            P("rep", None),
            P("rep", None),
            P("rep", None),
            P(None, "planes", None),
            P(),
            P(),
            P("wide", None, None),
            P("wide", None),
        ),
        out_specs=(
            P("planes", ("groups", "wide"), "rep"),
            P("planes", ("groups", "wide"), "rep", None),
        ),
        check_vma=False,
    )
```

```python
import functools

import jax
import jax.numpy as jnp
from jax import lax
from jax.experimental import pallas as pl
from jax.experimental.pallas import tpu as pltpu
from jax.sharding import PartitionSpec as P

MESH = pl.DeviceIdType.MESH
BF = jnp.bfloat16
F32 = jnp.float32


def banded(taps_ref, where_tap):
    out = jnp.zeros(where_tap.shape, F32)
    for k in range(taps_ref.shape[0]):
        out = jnp.where(where_tap == k, taps_ref[k], out)
    return out.astype(BF)


def lag_table(gain_ref, dil_ref, total):
    bands, _, taps = gain_ref.shape
    lag = lax.broadcasted_iota(jnp.int32, (1, 2 * total), 1) - (total - 1)
    row = jnp.zeros((1, 2 * total), F32)
    for b in range(bands):
        for k in range(taps):
            row = row + jnp.where(lag == dil_ref[0, b] * (k - (taps - 1) // 2), gain_ref[b, 0, k], 0.0)
    spread = jnp.broadcast_to(row, (total, 2 * total))
    return pltpu.roll(spread, total + 1, 1, stride=1, stride_axis=0)[:, :total].astype(BF)


def kernel(
    movie_ref, sup_ref, own_ref, table_ref, gain_ref, dil_ref, mask_ref, row_ref, col_ref,
    spad, tr_ref,
    temp_ref, hot, pall, part, xrecv, zsend, gath, lag_ref, lag_all, tbuf, tr_all, fold,
    top_in, bot_in, top_res, bot_res, cells, tr_rows, tr_out,
    lag_s, lag_r, x1_s, x1_r, z1_s, z1_r, z2_s, z2_r, x2_s, x2_r, h_s, h_r,
):
    np_ = lax.axis_size("planes")
    nw = lax.axis_size("wide")
    nr = lax.axis_size("rep")
    p = lax.axis_index("planes")
    z = lax.axis_index("wide")
    r = lax.axis_index("rep")
    blocks, hb, frames, comps = part.shape
    planes_here, _, rows, width = movie_ref.shape
    rim = (row_ref.shape[0] - 1) // 2
    edge = (spad.shape[2] - rows) // 2
    images = planes_here * frames
    shapes = temp_ref.shape[0]
    tile = min(256, shapes)
    total = nw * frames
    step = 4
    many = 8

    barrier = pltpu.get_barrier_semaphore()

    @pl.when(r > 0)
    def _():
        pl.semaphore_signal(barrier, inc=1, device_id={"rep": r - 1}, device_id_type=MESH)

    @pl.when(r < nr - 1)
    def _():
        pl.semaphore_signal(barrier, inc=1, device_id={"rep": r + 1}, device_id_type=MESH)

    for k in range(1, nw):
        pl.semaphore_signal(barrier, inc=1, device_id={"wide": lax.rem(z + k, nw)}, device_id_type=MESH)
    for k in range(1, np_):
        pl.semaphore_signal(barrier, inc=1, device_id={"planes": lax.rem(p + k, np_)}, device_id_type=MESH)

    lag_ref[...] = lag_table(gain_ref, dil_ref, total)
    lag_all[z] = lag_ref[...]
    inner = lax.broadcasted_iota(jnp.int32, (width, width), 0)
    outer = lax.broadcasted_iota(jnp.int32, (width, width), 1)
    col_fwd = banded(col_ref, inner - outer + rim)

    pl.semaphore_wait(barrier, nw - 1 + np_ - 1 + lax.min(r, 1) + lax.min(nr - 1 - r, 1))

    def halo(source, lo, hi, top, bot, base):
        down = pltpu.make_async_remote_copy(
            src_ref=source.at[:, :, hi : hi + edge], dst_ref=top,
            send_sem=h_s.at[base], recv_sem=h_r.at[base],
            device_id={"rep": lax.min(r + 1, nr - 1)}, device_id_type=MESH)
        up = pltpu.make_async_remote_copy(
            src_ref=source.at[:, :, lo : lo + edge], dst_ref=bot,
            send_sem=h_s.at[base + 1], recv_sem=h_r.at[base + 1],
            device_id={"rep": lax.max(r - 1, 0)}, device_id_type=MESH)
        return down, up

    def halo_start(copies):
        @pl.when(r < nr - 1)
        def _():
            copies[0].start()

        @pl.when(r > 0)
        def _():
            copies[1].start()

    def halo_finish(copies, top, bot):
        @pl.when(r > 0)
        def _():
            copies[0].wait_recv()
            copies[1].wait_send()

        @pl.when(r == 0)
        def _():
            top[...] = jnp.zeros_like(top)

        @pl.when(r < nr - 1)
        def _():
            copies[1].wait_recv()
            copies[0].wait_send()

        @pl.when(r == nr - 1)
        def _():
            bot[...] = jnp.zeros_like(bot)

    in_copies = halo(movie_ref, 0, rows - edge, top_in, bot_in, 0)
    halo_start(in_copies)
    for pi in range(planes_here):
        temp_ref[:, pi * width : (pi + 1) * width] = table_ref[:, pi, :]

    def to_wide(src, dst, send, recv, k):
        return pltpu.make_async_remote_copy(
            src_ref=src, dst_ref=dst, send_sem=send.at[k - 1], recv_sem=recv.at[k - 1],
            device_id={"wide": lax.rem(z + k, nw)}, device_id_type=MESH)

    def to_plane(src, dst, send, recv, dp, zi):
        slot = (dp - 1) * nw + zi
        return pltpu.make_async_remote_copy(
            src_ref=src, dst_ref=dst, send_sem=send.at[slot], recv_sem=recv.at[slot],
            device_id={"planes": lax.rem(p + dp, np_)}, device_id_type=MESH)

    def lag_copy(k):
        return to_wide(lag_ref, lag_all.at[z], lag_s, lag_r, k)

    def x1_copy(dp, zi):
        return to_plane(part.at[lax.rem(p + dp, np_) * nw + zi], xrecv.at[(dp - 1) * nw + zi], x1_s, x1_r, dp, zi)

    def z1_copy(k):
        return to_wide(zsend.at[lax.rem(z + k, nw)], gath.at[z], z1_s, z1_r, k)

    def z2_copy(k):
        return to_wide(tbuf.at[lax.rem(z + k, nw)], tr_all.at[p * nw + z], z2_s, z2_r, k)

    def x2_copy(dp, zi):
        return to_plane(tr_all.at[p * nw + zi], tr_all.at[p * nw + zi], x2_s, x2_r, dp, zi)

    for k in range(1, nw):
        lag_copy(k).start()

    def smooth(n, carry):
        pi, f = n * many // frames, lax.rem(n * many, frames)
        spad[pi, pl.ds(f, many), edge : edge + rows] = jnp.dot(
            movie_ref[pi, pl.ds(f, many)].reshape(many * rows, width), col_fwd, preferred_element_type=F32
        ).astype(BF).reshape(many, rows, width)
        return carry

    lax.fori_loop(0, images // many, smooth, 0)
    here = lax.broadcasted_iota(jnp.int32, (rows, rows + 2 * edge), 0)
    there = lax.broadcasted_iota(jnp.int32, (rows, rows + 2 * edge), 1) - edge
    row_fwd = banded(row_ref, there - here + rim)
    halo_finish(in_copies, top_in, bot_in)
    for pi in range(planes_here):
        for held, at in ((top_in, 0), (bot_in, edge + rows)):
            spad[pi, :, at : at + edge] = jnp.dot(
                held[pi].reshape(frames * edge, width), col_fwd, preferred_element_type=F32
            ).astype(BF).reshape(frames, edge, width)
    mask_all = mask_ref[...].reshape(rows, width).astype(F32)

    def along(n, carry):
        for u in range(0, many, 2):
            q = n * many + u
            pi, f = q // frames, lax.rem(q, frames)
            pair = jnp.concatenate([spad[pi, f], spad[pi, f + 1]], axis=1)
            value = jnp.dot(row_fwd, pair, preferred_element_type=F32)
            for v in range(2):
                cells[pi, pl.ds(f + v, rows, stride=frames), :] = (
                    value[:, v * width : (v + 1) * width] * mask_all)
        return carry

    lax.fori_loop(0, images // many, along, 0)

    def block_cells(b):
        span = pl.ds(b * hb * frames, hb * frames)
        return jnp.concatenate([cells[pi, span, :] for pi in range(planes_here)], axis=1).astype(BF)

    ids = lax.broadcasted_iota(jnp.int32, (tile, comps), 0).astype(F32).astype(BF)
    one, none = jnp.ones((), BF), jnp.zeros((), BF)

    def project(b):
        base = b * hb
        f_blk = block_cells(b)
        pall[...] = lax.dot_general(
            f_blk, temp_ref[...], (((1,), (1,)), ((), ())), preferred_element_type=F32).astype(BF)
        sup = sup_ref[b]
        for i in range(hb):
            row = sup[i : i + 1, :]
            marks = jnp.concatenate(
                [
                    jnp.where(ids == (row - q).astype(F32).astype(BF), one, none)
                    for q in range(0, shapes, tile)
                ],
                axis=0,
            )
            hot[base + i] = marks
            part[b, i] = jnp.dot(
                pall[i * frames : (i + 1) * frames, :], marks, preferred_element_type=F32).astype(BF)

    def others(n, carry):
        dp = n // nw + 1
        zi = lax.rem(z + 1 + n, nw)
        project(lax.rem(p + dp, np_) * nw + zi)
        x1_copy(dp, zi).start()
        return carry

    lax.fori_loop(0, (np_ - 1) * nw, others, 0)

    def mine(n, carry):
        zi = lax.rem(z + 1 + n, nw)
        b = p * nw + zi
        project(b)
        acc = part[b].astype(F32)
        for dp in range(1, np_):
            x1_copy(dp, zi).wait_recv()
            acc = acc + xrecv[(dp - 1) * nw + zi].astype(F32)
        zsend[zi] = acc.astype(BF)

        @pl.when(n < nw - 1)
        def _():
            z1_copy(n + 1).start()

        return carry

    lax.fori_loop(0, nw, mine, 0)
    gath[z] = zsend[z]

    def arrived(k, carry):
        lag_copy(k).wait()
        z1_copy(k).wait()
        return carry

    lax.fori_loop(1, nw, arrived, 0)

    me = p * nw + z
    for i in range(hb):
        table = lag_all[own_ref[me * hb + i]]
        columns = gath[:, i].reshape(total, comps)
        scores = jnp.dot(table, columns, preferred_element_type=F32)
        tbuf[:, i] = jnp.maximum(scores, 0.0).astype(BF).reshape(nw, frames, comps)

    def give(k, carry):
        z2_copy(k).start()
        return carry

    lax.fori_loop(1, nw, give, 0)
    tr_all[me] = tbuf[z]

    def model(b):
        base = b * hb
        for i in range(hb):
            fold[i * frames : (i + 1) * frames, :] = lax.dot_general(
                tr_all[b, i], hot[base + i], (((1,), (1,)), ((), ())), preferred_element_type=F32).astype(BF)
        tr_rows[pl.ds(base * frames, hb * frames), :] = tr_all[b].reshape(hb * frames, comps).astype(F32)
        out = jnp.dot(fold[...], temp_ref[...], preferred_element_type=F32)
        mask = mask_ref[b].astype(F32)
        mask = jnp.broadcast_to(mask[:, None, :], (hb, frames, width)).reshape(hb * frames, width)
        mask = jnp.concatenate([mask] * planes_here, axis=1)
        left = (block_cells(b).astype(F32) - mask * out).astype(BF).astype(F32)
        for pi in range(planes_here):
            cells[pi, pl.ds(base * frames, hb * frames), :] = left[:, pi * width : (pi + 1) * width]

    def same_plane(k, carry):
        zi = lax.rem(z + nw - k, nw)

        @pl.when(k > 0)
        def _():
            z2_copy(lax.max(k, 1)).wait_recv()

        for dp in range(1, np_):
            x2_copy(dp, zi).start()
        model(p * nw + zi)
        return carry

    lax.fori_loop(0, nw, same_plane, 0)

    def other_planes(n, carry):
        dp = n // nw + 1
        zi = lax.rem(z + nw - lax.rem(n, nw), nw)
        x2_copy(dp, zi).wait_recv()
        model(lax.rem(p + np_ - dp, np_) * nw + zi)
        return carry

    lax.fori_loop(0, (np_ - 1) * nw, other_planes, 0)

    def edges(n, carry):
        for u in range(step):
            q = n * step + u
            pi, f = q // frames, lax.rem(q, frames)
            for at in (0, rows - edge):
                spad[pi, f, edge + at : 2 * edge + at] = cells[
                    pi, pl.ds(f + at * frames, edge, stride=frames), :].astype(BF)
        return carry

    lax.fori_loop(0, images // step, edges, 0)
    out_copies = halo(spad, edge, rows, top_res, bot_res, 2)
    halo_start(out_copies)

    def inside(n, carry):
        for u in range(step):
            q = n * step + u
            pi, f = q // frames, lax.rem(q, frames)
            spad[pi, f, 2 * edge : rows] = cells[
                pi, pl.ds(f + edge * frames, rows - 2 * edge, stride=frames), :].astype(BF)
        return carry

    lax.fori_loop(0, images // step, inside, 0)

    share = comps // np_
    pick = (
        lax.broadcasted_iota(jnp.int32, (share, comps), 0) + p * share
        == lax.broadcasted_iota(jnp.int32, (share, comps), 1)
    )
    pick = jnp.where(pick, 1.0, 0.0).astype(BF)
    for t in range(frames):
        one = tr_rows[pl.ds(t, rows, stride=frames), :].astype(BF)
        tr_out[pl.ds(t, share, stride=frames), :] = lax.dot_general(
            pick, one, (((1,), (1,)), ((), ())), preferred_element_type=F32)
    tr_ref[...] = tr_out[...].astype(BF).reshape(tr_ref.shape)

    halo_finish(out_copies, top_res, bot_res)
    spad[:, :, 0:edge] = top_res[...]
    spad[:, :, edge + rows :] = bot_res[...]


    def drained_planes(n, carry):
        x1_copy(n // nw + 1, lax.rem(n, nw)).wait_send()
        x2_copy(n // nw + 1, lax.rem(n, nw)).wait_send()
        return carry

    lax.fori_loop(0, (np_ - 1) * nw, drained_planes, 0)

    def drained_wide(k, carry):
        z2_copy(k).wait_send()
        return carry

    lax.fori_loop(1, nw, drained_wide, 0)


def adjoint_kernel(rim, edge, pad_ref, tr_ref, row_ref, col_ref, back_ref, out_ref, row_adj, col_adj):
    rows, width = back_ref.shape[1:]

    @pl.when(pl.program_id(0) == 0)
    def _():
        here = lax.broadcasted_iota(jnp.int32, row_adj.shape, 0)
        there = lax.broadcasted_iota(jnp.int32, row_adj.shape, 1) - edge
        row_adj[...] = banded(row_ref, here - there + rim)
        inner = lax.broadcasted_iota(jnp.int32, (width, width), 0)
        outer = lax.broadcasted_iota(jnp.int32, (width, width), 1)
        col_adj[...] = banded(col_ref, outer - inner + rim)

    count = back_ref.shape[0]
    parts = []
    for q in range(0, count, 2):
        pair = jnp.concatenate([pad_ref[q], pad_ref[q + 1]], axis=1)
        value = jnp.dot(row_adj[...], pair, preferred_element_type=F32).astype(BF)
        parts += [value[:, :width], value[:, width:]]
    back_ref[...] = jnp.dot(
        jnp.concatenate(parts, axis=0), col_adj[...], preferred_element_type=F32
    ).astype(BF).reshape(count, rows, width)
    out_ref[...] = tr_ref[...]


def on_device(
    movie_frames, pixel_mask, tile_owner, support, templates, row_taps, col_taps, lag_gains, dilations
):
    np_ = lax.axis_size("planes")
    nw = lax.axis_size("wide")
    blocks = np_ * nw
    planes_here, frames, rows, width = movie_frames.shape
    hb = rows // blocks
    comps = support.shape[1]
    count = templates.shape[0]
    total = nw * frames
    rim = (row_taps.shape[0] - 1) // 2
    edge = -(-rim // 16) * 16
    vm = pl.BlockSpec(memory_space=pltpu.VMEM)
    sm = pl.BlockSpec(memory_space=pltpu.SMEM)
    dma = pltpu.SemaphoreType.DMA
    piece = (hb, frames, comps)
    across = (np_ - 1) * nw
    halo = pltpu.VMEM((planes_here, frames, edge, width), BF)
    padded = (planes_here * frames, rows + 2 * edge, width)
    held, traces = pl.pallas_call(
        kernel,
        out_shape=(
            jax.ShapeDtypeStruct((planes_here, frames) + padded[1:], BF),
            jax.ShapeDtypeStruct((comps // np_, frames, rows), BF),
        ),
        in_specs=[vm, vm, sm, vm, sm, sm, vm, sm, sm],
        out_specs=(vm, vm),
        scratch_shapes=[
            pltpu.VMEM((count, planes_here * width), BF),
            pltpu.VMEM((rows, count, comps), BF),
            pltpu.VMEM((hb * frames, count), BF),
            pltpu.VMEM((blocks,) + piece, BF),
            pltpu.VMEM((across,) + piece, BF),
            pltpu.VMEM((nw,) + piece, BF),
            pltpu.VMEM((nw,) + piece, BF),
            pltpu.VMEM((total, total), BF),
            pltpu.VMEM((nw, total, total), BF),
            pltpu.VMEM((nw,) + piece, BF),
            pltpu.VMEM((blocks,) + piece, BF),
            pltpu.VMEM((hb * frames, count), BF),
            halo, halo, halo, halo,
            pltpu.VMEM((planes_here, rows * frames, width), F32),
            pltpu.VMEM((rows * frames, comps), F32),
            pltpu.VMEM((comps // np_ * frames, rows), F32),
            dma((nw - 1,)), dma((nw - 1,)),
            dma((across,)), dma((across,)),
            dma((nw - 1,)), dma((nw - 1,)),
            dma((nw - 1,)), dma((nw - 1,)),
            dma((across,)), dma((across,)),
            dma((4,)), dma((4,)),
        ],
        compiler_params=pltpu.CompilerParams(
            collective_id=0, has_side_effects=True, vmem_limit_bytes=63 * 1024 * 1024
        ),
    )(
        movie_frames,
        support.reshape(blocks, hb, comps),
        tile_owner[:, 0],
        templates,
        jnp.transpose(lag_gains, (1, 0, 2)),
        dilations,
        pixel_mask.reshape(blocks, hb, width),
        row_taps,
        col_taps,
    )
    steps = frames // 2
    few = padded[0] // steps
    share = traces.shape[0] // steps if traces.shape[0] % steps == 0 else 0
    part_spec = pl.BlockSpec((share,) + traces.shape[1:], lambda i: (i, 0, 0))
    back, traces = pl.pallas_call(
        functools.partial(adjoint_kernel, rim, edge),
        grid=(steps,),
        out_shape=(
            jax.ShapeDtypeStruct((padded[0], rows, width), BF),
            jax.ShapeDtypeStruct(traces.shape, BF),
        ),
        in_specs=[
            pl.BlockSpec((few,) + padded[1:], lambda i: (i, 0, 0)),
            part_spec,
            sm,
            sm,
        ],
        out_specs=(pl.BlockSpec((few, rows, width), lambda i: (i, 0, 0)), part_spec),
        scratch_shapes=[pltpu.VMEM((rows, rows + 2 * edge), BF), pltpu.VMEM((width, width), BF)],
        compiler_params=pltpu.CompilerParams(vmem_limit_bytes=63 * 1024 * 1024),
    )(held.reshape(padded), traces, row_taps, col_taps)
    return (traces, back.reshape(movie_frames.shape))


def solution(mesh):
    return jax.shard_map(
        on_device,
        mesh=mesh,
        in_specs=(
            P("planes", ("groups", "wide"), "rep", None),
            P("rep", None),
            P("rep", None),
            P("rep", None),
            P(None, "planes", None),
            P(),
            P(),
            P("wide", None, None),
            P("wide", None),
        ),
        out_specs=(
            P("planes", ("groups", "wide"), "rep"),
            P("planes", ("groups", "wide"), "rep", None),
        ),
        check_vma=False,
    )
```
